32 devices in a mesh: facet: 8 (over z, x), strip: 4 (over y, core).
Axes of the slice: x: 2, y: 2, z: 4, core: 2. Of those that a mesh axis runs over, the one named last changes fastest.
Arguments:
- facets: bfloat16 [8, 2, 512, 8192], P('facet', None, None, 'strip'), may hold values from -6 to 6
- offsets: int32 [4], replicated, may hold values from 0 to 32767
- visibilities: float32 [2, 512, 2048], P(None, 'strip', 'facet'), may hold values from -24 to 24
- weights: float32 [512, 2048], P('strip', 'facet'), may hold values from 0.1 to 1
- mask: int32 [512, 2048], P('strip', 'facet'), may hold values 0 or 1
Outputs:
- facet_update: bfloat16 [8, 2, 512, 8192], P('facet', None, None, 'strip')
The draws below stay inside these ranges and needn't reach their ends.
Inputs may be any that keep to these rules, and one draw needn't show every extreme that they name: `mask`: 1 where the cell holds a sampled visibility.
All inputs are finite; a program needn't handle non-finite values. No bound on the sum of `mask` on one device may be relied on, other than what follows from the above.
Results may differ from the reference program's by a relative error of at most 0.0058.
Values may be sent and summed in bfloat16 or wider, within the bound.
No kernel may reach another device: no remote copies, remote signals or barrier semaphores. Data moves between devices by JAX's collectives and lax.ppermute only.
A program may use at most 128 MiB of HBM per device.

```python
import math
import jax
import jax.numpy as jnp
from jax import lax

NG = 32768
XM = 8192
SG = 512
NSUB = 4
FROWS = 4
NF = 8
NK = 2048


def place_ends(drawn, stream_key, low, largest):
    dims = drawn.shape
    index_at = [jax.random.randint(jax.random.fold_in(stream_key, axis), (), 0, dims[axis]) for axis in range(len(dims))]
    drawn = drawn.at[tuple(index_at)].set(low)
    longest = dims.index(max(dims))
    index_at[longest] = (index_at[longest] + 1) % dims[longest]
    return drawn.at[tuple(index_at)].set(largest)


def block_scale(own_key, dims, cuts, low, largest):
    gain, own = 1.0, jax.random.fold_in(own_key, 6)
    for position, shards_of in cuts:
        heights = jnp.exp(jax.random.uniform(jax.random.fold_in(own, position), (shards_of,), jnp.float32, low / len(cuts), largest / len(cuts)))
        gain = gain * jnp.repeat(heights, dims[position] // shards_of).reshape([-1 if axis == position else 1 for axis in range(len(dims))])
    return gain


def bell_draw(stream_key, shape, deviation, limit, split=(), held_as=jnp.bfloat16):
    level = block_scale(stream_key, shape, split, -0.22, 0.18) if split else 1.0
    array = jax.random.normal(stream_key, shape, jnp.float32) * deviation * level
    return jnp.minimum(jnp.maximum(array, -limit), limit).astype(held_as)


def setup_inputs(seed: int = 0) -> dict:
    arg_keys = jax.random.split(jax.random.key(seed), 6)
    return {
        "facets": bell_draw(arg_keys[0], (NF, 2, SG, XM), 1.0, 6.0, ((0, 8), (3, 4))),
        "offsets": place_ends(jax.random.randint(arg_keys[1], (NSUB,), 0, NG), jax.random.fold_in(arg_keys[1], 1), 0, NG - 1).astype(jnp.int32),
        "visibilities": bell_draw(arg_keys[2], (2, SG, NK), 4.0, 24.0, ((1, 4), (2, 8)), jnp.float32),
        "weights": jnp.clip(jnp.exp(math.log(1.0) - 2.3025851 * jax.random.uniform(arg_keys[3], (SG, NK), jnp.float32) ** block_scale(arg_keys[3], (SG, NK), ((0, 4), (1, 8)), -0.2, 0.2)), 0.1, 1.0),
        "mask": place_ends((jax.random.randint(arg_keys[4], (SG, NK), 0, 2) < 1).astype(jnp.int32), jax.random.fold_in(arg_keys[4], 1), 0, 1),
    }


def residue_angle(count):
    return count.astype(jnp.float32) * (2.0 * math.pi / NG)

def dft_kernel(start, rows):
    positions = start + jnp.arange(rows, dtype=jnp.int32)
    cells = jnp.arange(SG, dtype=jnp.int32)
    angle = residue_angle(positions[:, None] * cells[None, :] % NG)
    return jnp.concatenate([jnp.cos(angle), jnp.sin(angle)], axis=1).astype(jnp.bfloat16)

def row_angles(start, rows, offsets):
    positions = start + jnp.arange(rows, dtype=jnp.int32)
    return residue_angle(offsets[:, None] * positions[None, :] % NG)

def column_angles(facet_index, offsets):
    centre = (facet_index % FROWS * XM + NG // 2) % NG
    cells = jnp.arange(SG, dtype=jnp.int32)
    return residue_angle((cells[None, :] * centre % NG + offsets[:, None] * centre % NG) % NG)

def forward(data, start, facet_index, offsets, kernel_table):
    columns = data.shape[1]
    rows = data.shape[2]
    phi = row_angles(start, rows, offsets)[:, None, :]
    cos_phi = jnp.cos(phi)
    sin_phi = jnp.sin(phi)
    real_part = data[0].astype(jnp.float32)[None]
    imag_part = data[1].astype(jnp.float32)[None]
    twisted = jnp.stack([real_part * cos_phi + imag_part * sin_phi, imag_part * cos_phi - real_part * sin_phi], axis=1).astype(jnp.bfloat16)
    spectra = jnp.dot(twisted.reshape(-1, rows), kernel_table, preferred_element_type=jnp.float32)
    spectra = spectra.reshape(NSUB, 2, columns, 2, SG)
    spectrum_real = spectra[:, 0, :, 0] + spectra[:, 1, :, 1]
    spectrum_imag = spectra[:, 1, :, 0] - spectra[:, 0, :, 1]
    psi = column_angles(facet_index, offsets)[:, None, :]
    cos_psi = jnp.cos(psi)
    sin_psi = jnp.sin(psi)
    scale = 1.0 / math.sqrt(XM)
    result_real = (spectrum_real * cos_psi + spectrum_imag * sin_psi) * scale
    result_imag = (spectrum_imag * cos_psi - spectrum_real * sin_psi) * scale
    stacked = jnp.stack([result_real, result_imag])
    return stacked.transpose(0, 2, 1, 3).reshape(2, columns, NSUB * SG)

def adjoint(residual, start, facet_index, offsets, kernel_table):
    columns = residual.shape[1]
    rows = kernel_table.shape[0]
    values = residual.astype(jnp.float32).reshape(2, columns, NSUB, SG).transpose(0, 2, 1, 3)
    psi = column_angles(facet_index, offsets)[:, None, :]
    cos_psi = jnp.cos(psi)
    sin_psi = jnp.sin(psi)
    first = values[0] * cos_psi - values[1] * sin_psi
    second = values[1] * cos_psi + values[0] * sin_psi
    untwisted = jnp.stack([first, second], axis=1).astype(jnp.bfloat16)
    images = jnp.einsum('mj,xpj->pmx', untwisted.reshape(-1, SG).astype(jnp.float32), kernel_table.reshape(rows, 2, SG).astype(jnp.float32))
    images = images.reshape(2, NSUB, 2, columns, rows)
    image_real = images[0, :, 0] - images[1, :, 1]
    image_imag = images[0, :, 1] + images[1, :, 0]
    phi = row_angles(start, rows, offsets)[:, None, :]
    cos_phi = jnp.cos(phi)
    sin_phi = jnp.sin(phi)
    scale = 1.0 / math.sqrt(XM)
    total_real = lax.optimization_barrier(jnp.sum(image_real * cos_phi - image_imag * sin_phi, axis=0)) * scale
    total_imag = lax.optimization_barrier(jnp.sum(image_imag * cos_phi + image_real * sin_phi, axis=0)) * scale
    return jnp.stack([total_real, total_imag])

def reference(facets, offsets, visibilities, weights, mask):
    kernel_table = dft_kernel(0, XM)
    facet_ids = jnp.arange(NF, dtype=jnp.int32)

    def one_facet(carry, item):
        index, data = item
        return (carry + forward(data, 0, index, offsets, kernel_table), None)
    model, _ = lax.scan(one_facet, jnp.zeros((2, SG, NSUB * SG), jnp.float32), (facet_ids, facets))
    factor = weights * mask.astype(jnp.float32)
    residual = (factor[None] * (visibilities - model)).astype(jnp.bfloat16)

    def back_facet(index):
        return adjoint(residual, 0, index, offsets, kernel_table).astype(jnp.bfloat16)
    return lax.map(back_facet, facet_ids)
```

```python
import functools
import math

import jax
import jax.numpy as jnp
from jax import lax
from jax.experimental import pallas as pl
from jax.experimental.pallas import tpu as pltpu
from jax.sharding import PartitionSpec as P

NG = 32768
FROWS = 4
FINE = 32
AXES = ("facet", "strip")
bf16 = jnp.bfloat16
f32 = jnp.float32


def unit_circle(count):
    count = count & (NG - 1)
    quarter = (count + NG // 8) >> (NG.bit_length() - 3)
    angle = (count - quarter * (NG // 4)).astype(f32) * (2.0 * math.pi / NG)
    square = angle * angle
    sine = angle * (
        1.0 + square * (-1.0 / 6 + square * (1.0 / 120 + square * (-1.0 / 5040 + square * (1.0 / 362880))))
    )
    cosine = 1.0 + square * (
        -0.5 + square * (1.0 / 24 + square * (-1.0 / 720 + square * (1.0 / 40320 + square * (-1.0 / 3628800))))
    )
    odd = (quarter & 1) == 1
    first = jnp.where(odd, sine, cosine)
    second = jnp.where(odd, cosine, sine)
    return (
        jnp.where(((quarter + 1) & 2) != 0, -first, first),
        jnp.where((quarter & 2) != 0, -second, second),
    )


class Layout:
    def __init__(self, mesh):
        self.strips = mesh.shape["strip"]
        self.facets = mesh.shape["facet"]
        self.cores = 2 if self.strips % 2 == 0 else 1
        self.high = self.strips // self.cores
        self.near = 2 if self.facets % 2 == 0 else 1
        self.far = self.facets // self.near
        self.mixed = self.high == self.near and self.cores == 2

    def place(self):
        strip = lax.axis_index("strip")
        facet = lax.axis_index("facet")
        return strip // self.cores, strip % self.cores, facet // self.near, facet % self.near

    def permutation(self, move):
        pairs = []
        for facet in range(self.facets):
            for strip in range(self.strips):
                digits = move(strip // self.cores, strip % self.cores, facet // self.near, facet % self.near)
                high, core, far, near = digits
                target = (far * self.near + near) * self.strips + high * self.cores + core
                pairs.append((facet * self.strips + strip, target))
        return pairs

    def along(self, stage, shift):
        def move(high, core, far, near):
            if stage == "core":
                return high, (core + shift) % self.cores, far, near
            if stage == "far":
                return high, core, (far + shift) % self.far, near
            first = "near" if self.mixed and core == 1 else "high"
            second = "high" if first == "near" else "near"
            if (first if stage == "first" else second) == "high":
                return (high + shift) % self.high, core, far, near
            return high, core, far, (near + shift) % self.near

        return self.permutation(move)

    def send(self, value, stage, shift):
        return lax.ppermute(value, AXES, self.along(stage, shift))


def forward_kernel(lay, scale, info, *refs):
    if lay.cores == 2:
        away_in, keep_in, away_out, keep_out, cos_ref, sin_ref = refs
        halves = ((away_in, away_out, 1 - info[1]), (keep_in, keep_out, info[1]))
    else:
        keep_in, keep_out, cos_ref, sin_ref = refs
        halves = ((keep_in, keep_out, info[1]),)
    tile = pl.program_id(0)
    rows, width = cos_ref.shape
    cells = (pl.num_programs(0) * width) // info_offsets(info)
    start = tile * width
    offset = info[2 + start // cells]
    frequency = offset + start % cells + lax.broadcasted_iota(jnp.int32, (1, width), 1)
    coarse_rows = info[0] + FINE * lax.broadcasted_iota(jnp.int32, (rows // FINE, 1), 0)
    fine_rows = lax.broadcasted_iota(jnp.int32, (FINE, 1), 0)
    frequency = frequency & (NG - 1)
    coarse_cos, coarse_sin = unit_circle((coarse_rows & (NG - 1)) * frequency)
    fine_cos, fine_sin = unit_circle(fine_rows * frequency)
    for block in range(rows // FINE):
        c = coarse_cos[block : block + 1]
        s = coarse_sin[block : block + 1]
        cos_ref[block * FINE : (block + 1) * FINE] = (c * fine_cos - s * fine_sin).astype(bf16)
        sin_ref[block * FINE : (block + 1) * FINE] = (s * fine_cos + c * fine_sin).astype(bf16)
    near = lax.rem(tile, lay.near)
    for data, out, core in halves:
        high, depth = data.shape[1], data.shape[-2]
        values = data[...].reshape(2 * high * depth, rows)
        with_cos = jnp.dot(values, cos_ref[...], preferred_element_type=f32).reshape(2, high, depth, width)
        with_sin = jnp.dot(values, sin_ref[...], preferred_element_type=f32).reshape(2, high, depth, width)
        real = ((with_cos[0] + with_sin[1]) * scale).astype(bf16)
        imag = ((with_cos[1] - with_sin[0]) * scale).astype(bf16)
        for h in range(high):
            spot = h * lay.near + near
            if lay.mixed:
                spot = jnp.where(core == 1, near * lay.high + h, spot)
            out[spot, 0, 0] = real[h]
            out[spot, 0, 1] = imag[h]


def info_offsets(info):
    return info.shape[0] - 2


def forward(lay, data, info, chunk, chunks, width, scale):
    rows = data.shape[-1]
    depth = data.shape[3] // chunks
    tiles = lay.facets
    half = (2, lay.high, None, depth, rows)
    out_block = (lay.high * lay.near, 1, 2, depth, width)
    out_shape = jax.ShapeDtypeStruct((lay.high * lay.near, lay.far, 2, depth, width), bf16)
    out_spec = pl.BlockSpec(out_block, lambda t, info: (0, t // lay.near, 0, 0, 0))
    table_shape = jax.ShapeDtypeStruct((rows, tiles * width), bf16)
    table_spec = pl.BlockSpec((rows, width), lambda t, info: (0, t))
    in_specs = [pl.BlockSpec(half, lambda t, info: (0, 0, info[1], chunk, 0))]
    if lay.cores == 2:
        in_specs.insert(0, pl.BlockSpec(half, lambda t, info: (0, 0, 1 - info[1], chunk, 0)))
    n = len(in_specs)
    return pl.pallas_call(
        functools.partial(forward_kernel, lay, scale),
        out_shape=(out_shape,) * n + (table_shape,) * 2,
        grid_spec=pltpu.PrefetchScalarGridSpec(
            num_scalar_prefetch=1,
            grid=(tiles,),
            in_specs=in_specs,
            out_specs=(out_spec,) * n + (table_spec,) * 2,
        ),
        compiler_params=pltpu.CompilerParams(vmem_limit_bytes=58 << 20),
        name="forward",
    )(info, *([data] * n))


def adjoint_kernel(lay, scale, place, *refs):
    sources = refs[: lay.cores]
    cos_ref, sin_ref, out_ref, left = refs[lay.cores :]
    width = sources[0].shape[-1]
    depth = sources[0].shape[-2]

    @pl.when(pl.program_id(0) == 0)
    def _():
        for i, source in enumerate(sources):
            core = place[1] if i == 0 else 1 - place[1]
            for first in range(source.shape[0]):
                for second in range(source.shape[1]):
                    shifts = (first, second)
                    high = lax.rem(place[0] - shifts[0] + lay.high, lay.high)
                    near = lax.rem(place[3] - shifts[1] + lay.near, lay.near)
                    if lay.mixed:
                        high = jnp.where(core == 1, lax.rem(place[0] - second + lay.high, lay.high), high)
                        near = jnp.where(core == 1, lax.rem(place[3] - first + lay.near, lay.near), near)
                    for third in range(lay.far):
                        far = lax.rem(place[2] - third + lay.far, lay.far)
                        spot = pl.multiple_of((far * lay.near + near) * width, width)
                        for part in range(2):
                            left[i, part, high, :, pl.ds(spot, width)] = source[first, second, third, part]

    for i in range(len(sources)):
        core = place[1] if i == 0 else 1 - place[1]
        values = left[i].reshape(2 * lay.high * depth, left.shape[-1])
        contract = (((1,), (1,)), ((), ()))
        with_cos = lax.dot_general(values, cos_ref[...], contract, preferred_element_type=f32)
        with_sin = lax.dot_general(values, sin_ref[...], contract, preferred_element_type=f32)
        shape = (2, lay.high, depth, with_cos.shape[-1])
        with_cos, with_sin = with_cos.reshape(shape), with_sin.reshape(shape)
        real = ((with_cos[0] - with_sin[1]) * scale).astype(bf16)
        imag = ((with_cos[1] + with_sin[0]) * scale).astype(bf16)
        for h in range(lay.high):
            out_ref[0, h, core] = real[h]
            out_ref[1, h, core] = imag[h]


def adjoint(lay, sources, cos_table, sin_table, place, shape, chunk, chunks, scale):
    rows, total = cos_table.shape
    depth = shape[3] // chunks
    tile = 256 if rows % 256 == 0 else rows
    source_spec = pl.BlockSpec(sources[0].shape, lambda t, place: (0,) * 6)
    table_spec = pl.BlockSpec((tile, total), lambda t, place: (t, 0))
    return pl.pallas_call(
        functools.partial(adjoint_kernel, lay, scale),
        out_shape=jax.ShapeDtypeStruct(shape, bf16),
        grid_spec=pltpu.PrefetchScalarGridSpec(
            num_scalar_prefetch=1,
            grid=(rows // tile,),
            in_specs=[source_spec] * len(sources) + [table_spec] * 2,
            out_specs=pl.BlockSpec((2, lay.high, lay.cores, depth, tile), lambda t, place: (0, 0, 0, chunk, t)),
            scratch_shapes=[pltpu.VMEM((len(sources), 2, lay.high, depth, total), bf16)],
        ),
        compiler_params=pltpu.CompilerParams(vmem_limit_bytes=58 << 20),
        name="adjoint",
    )(place, *sources, cos_table, sin_table)


def pick(value, index):
    return lax.dynamic_index_in_dim(value, index, 0, keepdims=False)


def total_of(*values):
    return functools.reduce(jnp.add, [v.astype(f32) for v in values])


def scatter_stage(lay, value, stage, size, mine):
    received = [
        lay.send(pick(value, lax.rem(mine + shift, size)), stage, shift) for shift in range(1, size)
    ]
    return total_of(pick(value, mine), *received)


def gather_stage(lay, value, stage, size):
    return jnp.stack([value] + [lay.send(value, stage, shift) for shift in range(1, size)])


def on_device(lay, facets, offsets, visibilities, weights, mask):
    high, core, far, near = lay.place()
    _, _, columns, rows = facets.shape
    width = visibilities.shape[2]
    own_columns = visibilities.shape[1]
    facet_index = lax.axis_index("facet")
    all_rows = rows * lay.strips
    base = lax.axis_index("strip") * rows + facet_index % FROWS * all_rows + NG // 2
    info = jnp.concatenate([jnp.stack([base, core]).astype(jnp.int32), offsets])
    place = jnp.stack([high, core, far, near]).astype(jnp.int32)
    scale = 1.0 / math.sqrt(all_rows)
    data = facets.reshape(2, lay.high, lay.cores, own_columns, rows)
    *partial, cos_table, sin_table = forward(lay, data, info, 0, 1, width, scale)
    value = partial[-1]
    if lay.cores == 2:
        value = total_of(value, lay.send(partial[0], "core", 1)).astype(bf16)
    sizes = (lay.high, lay.near)
    digits = (high, near)
    if lay.mixed:
        digits = (jnp.where(core == 1, near, high), jnp.where(core == 1, high, near))
    value = value.reshape(*sizes, *value.shape[1:])
    value = scatter_stage(lay, value, "first", sizes[0], digits[0]).astype(bf16)
    value = scatter_stage(lay, value, "second", sizes[1], digits[1]).astype(bf16)
    model = scatter_stage(lay, value, "far", lay.far, far)
    factor = weights * mask.astype(f32)
    residual = (factor[None] * (visibilities - model)).astype(bf16)
    value = gather_stage(lay, residual, "far", lay.far)
    value = gather_stage(lay, value, "second", sizes[1])
    value = gather_stage(lay, value, "first", sizes[0])
    sources = [value]
    if lay.cores == 2:
        sources.append(lay.send(value, "core", 1))
    update = adjoint(lay, sources, cos_table, sin_table, place, data.shape, 0, 1, scale)
    return update.reshape(facets.shape)


def solution(mesh):
    placed = (
        P("facet", None, None, "strip"),
        P(),
        P(None, "strip", "facet"),
        P("strip", "facet"),
        P("strip", "facet"),
    )
    return jax.shard_map(
        functools.partial(on_device, Layout(mesh)),
        mesh=mesh,
        in_specs=placed,
        out_specs=P("facet", None, None, "strip"),
        check_vma=False,
    )
```

```python
import functools
import math

import jax
import jax.numpy as jnp
from jax import lax
from jax.experimental import pallas as pl
from jax.experimental.pallas import tpu as pltpu
from jax.sharding import PartitionSpec as P


NG = 32768
FROWS = 4
FINE = 32
AXES = ("facet", "strip")
bf16 = jnp.bfloat16
f32 = jnp.float32


def unit_circle(count):
    count = count & (NG - 1)
    quarter = (count + NG // 8) >> (NG.bit_length() - 3)
    angle = (count - quarter * (NG // 4)).astype(f32) * (2.0 * math.pi / NG)
    square = angle * angle
    sine = angle * (
        1.0 + square * (-1.0 / 6 + square * (1.0 / 120 + square * (-1.0 / 5040 + square * (1.0 / 362880))))
    )
    cosine = 1.0 + square * (
        -0.5 + square * (1.0 / 24 + square * (-1.0 / 720 + square * (1.0 / 40320 + square * (-1.0 / 3628800))))
    )
    odd = (quarter & 1) == 1
    first = jnp.where(odd, sine, cosine)
    second = jnp.where(odd, cosine, sine)
    return (
        jnp.where(((quarter + 1) & 2) != 0, -first, first),
        jnp.where((quarter & 2) != 0, -second, second),
    )


class Layout:
    def __init__(self, mesh):
        self.strips = mesh.shape["strip"]
        self.facets = mesh.shape["facet"]
        self.cores = 2 if self.strips % 2 == 0 else 1
        self.high = self.strips // self.cores
        self.near = 2 if self.facets % 2 == 0 else 1
        self.far = self.facets // self.near
        self.mixed = self.high == self.near and self.cores == 2
        self.fast = self.mixed and self.high == 2

    def place(self):
        strip = lax.axis_index("strip")
        facet = lax.axis_index("facet")
        return strip // self.cores, strip % self.cores, facet // self.near, facet % self.near

    def permutation(self, move):
        pairs = []
        for facet in range(self.facets):
            for strip in range(self.strips):
                digits = move(strip // self.cores, strip % self.cores, facet // self.near, facet % self.near)
                high, core, far, near = digits
                target = (far * self.near + near) * self.strips + high * self.cores + core
                pairs.append((facet * self.strips + strip, target))
        return pairs

    def along(self, stage, shift):
        def move(high, core, far, near):
            if stage == "core":
                return high, (core + shift) % self.cores, far, near
            if stage == "far":
                return high, core, (far + shift) % self.far, near
            first = "near" if self.mixed and core == 1 else "high"
            second = "high" if first == "near" else "near"
            if (first if stage == "first" else second) == "high":
                return (high + shift) % self.high, core, far, near
            return high, core, far, (near + shift) % self.near

        return self.permutation(move)

    def send(self, value, stage, shift):
        return lax.ppermute(value, AXES, self.along(stage, shift))


def forward_kernel(lay, scale, info, *refs):
    if lay.cores == 2:
        away_in, keep_in, away_out, keep_out, cos_ref, sin_ref = refs
        halves = ((away_in, away_out, 1 - info[1]), (keep_in, keep_out, info[1]))
    else:
        keep_in, keep_out, cos_ref, sin_ref = refs
        halves = ((keep_in, keep_out, info[1]),)
    tile = pl.program_id(0)
    rows, width = cos_ref.shape
    cells = (pl.num_programs(0) * width) // info_offsets(info)
    start = tile * width
    offset = info[2 + start // cells]
    frequency = offset + start % cells + lax.broadcasted_iota(jnp.int32, (1, width), 1)
    coarse_rows = info[0] + FINE * lax.broadcasted_iota(jnp.int32, (rows // FINE, 1), 0)
    fine_rows = lax.broadcasted_iota(jnp.int32, (FINE, 1), 0)
    frequency = frequency & (NG - 1)
    coarse_cos, coarse_sin = unit_circle((coarse_rows & (NG - 1)) * frequency)
    fine_cos, fine_sin = unit_circle(fine_rows * frequency)
    for block in range(rows // FINE):
        c = coarse_cos[block : block + 1]
        s = coarse_sin[block : block + 1]
        cos_ref[block * FINE : (block + 1) * FINE] = (c * fine_cos - s * fine_sin).astype(bf16)
        sin_ref[block * FINE : (block + 1) * FINE] = (s * fine_cos + c * fine_sin).astype(bf16)
    near = lax.rem(tile, lay.near)
    for data, out, core in halves:
        high, depth = data.shape[1], data.shape[-2]
        values = data[...].reshape(2 * high * depth, rows)
        with_cos = jnp.dot(values, cos_ref[...], preferred_element_type=f32).reshape(2, high, depth, width)
        with_sin = jnp.dot(values, sin_ref[...], preferred_element_type=f32).reshape(2, high, depth, width)
        real = ((with_cos[0] + with_sin[1]) * scale).astype(bf16)
        imag = ((with_cos[1] - with_sin[0]) * scale).astype(bf16)
        for h in range(high):
            spot = h * lay.near + near
            if lay.mixed:
                spot = jnp.where(core == 1, near * lay.high + h, spot)
            out[spot, 0, 0] = real[h]
            out[spot, 0, 1] = imag[h]


def info_offsets(info):
    return info.shape[0] - 2


def forward(lay, data, info, chunk, chunks, width, scale):
    rows = data.shape[-1]
    depth = data.shape[3] // chunks
    tiles = lay.facets
    half = (2, lay.high, None, depth, rows)
    out_block = (lay.high * lay.near, 1, 2, depth, width)
    out_shape = jax.ShapeDtypeStruct((lay.high * lay.near, lay.far, 2, depth, width), bf16)
    out_spec = pl.BlockSpec(out_block, lambda t, info: (0, t // lay.near, 0, 0, 0))
    table_shape = jax.ShapeDtypeStruct((rows, tiles * width), bf16)
    table_spec = pl.BlockSpec((rows, width), lambda t, info: (0, t))
    in_specs = [pl.BlockSpec(half, lambda t, info: (0, 0, info[1], chunk, 0))]
    if lay.cores == 2:
        in_specs.insert(0, pl.BlockSpec(half, lambda t, info: (0, 0, 1 - info[1], chunk, 0)))
    n = len(in_specs)
    return pl.pallas_call(
        functools.partial(forward_kernel, lay, scale),
        out_shape=(out_shape,) * n + (table_shape,) * 2,
        grid_spec=pltpu.PrefetchScalarGridSpec(
            num_scalar_prefetch=1,
            grid=(tiles,),
            in_specs=in_specs,
            out_specs=(out_spec,) * n + (table_spec,) * 2,
        ),
        compiler_params=pltpu.CompilerParams(vmem_limit_bytes=58 << 20),
        name="forward",
    )(info, *([data] * n))


def adjoint_kernel(lay, scale, place, *refs):
    sources = refs[: lay.cores]
    cos_ref, sin_ref, out_ref, left = refs[lay.cores :]
    width = sources[0].shape[-1]
    depth = sources[0].shape[-2]

    @pl.when(pl.program_id(0) == 0)
    def _():
        for i, source in enumerate(sources):
            core = place[1] if i == 0 else 1 - place[1]
            for first in range(source.shape[0]):
                for second in range(source.shape[1]):
                    shifts = (first, second)
                    high = lax.rem(place[0] - shifts[0] + lay.high, lay.high)
                    near = lax.rem(place[3] - shifts[1] + lay.near, lay.near)
                    if lay.mixed:
                        high = jnp.where(core == 1, lax.rem(place[0] - second + lay.high, lay.high), high)
                        near = jnp.where(core == 1, lax.rem(place[3] - first + lay.near, lay.near), near)
                    for third in range(lay.far):
                        far = lax.rem(place[2] - third + lay.far, lay.far)
                        spot = pl.multiple_of((far * lay.near + near) * width, width)
                        for part in range(2):
                            left[i, part, high, :, pl.ds(spot, width)] = source[first, second, third, part]

    for i in range(len(sources)):
        core = place[1] if i == 0 else 1 - place[1]
        values = left[i].reshape(2 * lay.high * depth, left.shape[-1])
        contract = (((1,), (1,)), ((), ()))
        with_cos = lax.dot_general(values, cos_ref[...], contract, preferred_element_type=f32)
        with_sin = lax.dot_general(values, sin_ref[...], contract, preferred_element_type=f32)
        shape = (2, lay.high, depth, with_cos.shape[-1])
        with_cos, with_sin = with_cos.reshape(shape), with_sin.reshape(shape)
        real = ((with_cos[0] - with_sin[1]) * scale).astype(bf16)
        imag = ((with_cos[1] + with_sin[0]) * scale).astype(bf16)
        for h in range(lay.high):
            out_ref[0, h, core] = real[h]
            out_ref[1, h, core] = imag[h]


def adjoint(lay, sources, cos_table, sin_table, place, shape, chunk, chunks, scale):
    rows, total = cos_table.shape
    depth = shape[3] // chunks
    tile = 256 if rows % 256 == 0 else rows
    source_spec = pl.BlockSpec(sources[0].shape, lambda t, place: (0,) * 6)
    table_spec = pl.BlockSpec((tile, total), lambda t, place: (t, 0))
    return pl.pallas_call(
        functools.partial(adjoint_kernel, lay, scale),
        out_shape=jax.ShapeDtypeStruct(shape, bf16),
        grid_spec=pltpu.PrefetchScalarGridSpec(
            num_scalar_prefetch=1,
            grid=(rows // tile,),
            in_specs=[source_spec] * len(sources) + [table_spec] * 2,
            out_specs=pl.BlockSpec((2, lay.high, lay.cores, depth, tile), lambda t, place: (0, 0, 0, chunk, t)),
            scratch_shapes=[pltpu.VMEM((len(sources), 2, lay.high, depth, total), bf16)],
        ),
        compiler_params=pltpu.CompilerParams(vmem_limit_bytes=58 << 20),
        name="adjoint",
    )(place, *sources, cos_table, sin_table)


def pick(value, index):
    return lax.dynamic_index_in_dim(value, index, 0, keepdims=False)


def total_of(*values):
    return functools.reduce(jnp.add, [v.astype(f32) for v in values])


def scatter_stage(lay, value, stage, size, mine):
    received = [
        lay.send(pick(value, lax.rem(mine + shift, size)), stage, shift) for shift in range(1, size)
    ]
    return total_of(pick(value, mine), *received)


def gather_stage(lay, value, stage, size):
    return jnp.stack([value] + [lay.send(value, stage, shift) for shift in range(1, size)])


def in_stages(lay, facets, offsets, visibilities, weights, mask):
    high, core, far, near = lay.place()
    _, _, _, rows = facets.shape
    width = visibilities.shape[2]
    own_columns = visibilities.shape[1]
    facet_index = lax.axis_index("facet")
    all_rows = rows * lay.strips
    base = lax.axis_index("strip") * rows + facet_index % FROWS * all_rows + NG // 2
    info = jnp.concatenate([jnp.stack([base, core]).astype(jnp.int32), offsets])
    place = jnp.stack([high, core, far, near]).astype(jnp.int32)
    scale = 1.0 / math.sqrt(all_rows)
    data = facets.reshape(2, lay.high, lay.cores, own_columns, rows)
    *partial, cos_table, sin_table = forward(lay, data, info, 0, 1, width, scale)
    value = partial[-1]
    if lay.cores == 2:
        value = total_of(value, lay.send(partial[0], "core", 1)).astype(bf16)
    sizes = (lay.high, lay.near)
    digits = (high, near)
    if lay.mixed:
        digits = (jnp.where(core == 1, near, high), jnp.where(core == 1, high, near))
    value = value.reshape(*sizes, *value.shape[1:])
    value = scatter_stage(lay, value, "first", sizes[0], digits[0]).astype(bf16)
    value = scatter_stage(lay, value, "second", sizes[1], digits[1]).astype(bf16)
    model = scatter_stage(lay, value, "far", lay.far, far)
    factor = weights * mask.astype(f32)
    residual = (factor[None] * (visibilities - model)).astype(bf16)
    value = gather_stage(lay, residual, "far", lay.far)
    value = gather_stage(lay, value, "second", sizes[1])
    value = gather_stage(lay, value, "first", sizes[0])
    sources = [value]
    if lay.cores == 2:
        sources.append(lay.send(value, "core", 1))
    update = adjoint(lay, sources, cos_table, sin_table, place, data.shape, 0, 1, scale)
    return update.reshape(facets.shape)


WHOLE = pl.BlockSpec(memory_space=pltpu.VMEM)
SCALARS = pl.BlockSpec(memory_space=pltpu.SMEM)


def table_tile(lay, info, place, cos_ref, sin_ref, near, far, width):
    rows = cos_ref.shape[1]
    cells = lay.facets * width // info_offsets(info)
    digit = place[3] if near == 1 else 1 - place[3]
    coarse_rows = info[0] + FINE * lax.broadcasted_iota(jnp.int32, (rows // FINE, 1), 0)
    coarse_rows = coarse_rows & (NG - 1)
    fine_rows = lax.broadcasted_iota(jnp.int32, (FINE, 1), 0)
    start = (far * lay.near + digit) * width
    frequency = info[2 + start // cells] + start % cells + lax.broadcasted_iota(jnp.int32, (1, width), 1)
    frequency = frequency & (NG - 1)
    coarse_cos, coarse_sin = unit_circle(coarse_rows * frequency)
    fine_cos, fine_sin = unit_circle(fine_rows * frequency)
    spot = slice(far * width, (far + 1) * width)
    for block in range(rows // FINE):
        c = coarse_cos[block : block + 1]
        s = coarse_sin[block : block + 1]
        place_rows = slice(block * FINE, (block + 1) * FINE)
        cos_ref[near, place_rows, spot] = (c * fine_cos - s * fine_sin).astype(bf16)
        sin_ref[near, place_rows, spot] = (s * fine_cos + c * fine_sin).astype(bf16)


LIMIT = 8 << 20


def turned(values, cosine, sine, scale):
    half = values.shape[0] // 2
    with_cos = jnp.dot(values, cosine, preferred_element_type=f32)
    with_sin = jnp.dot(values, sine, preferred_element_type=f32)
    real = ((with_cos[:half] + with_sin[half:]) * scale).astype(bf16)
    imag = ((with_cos[half:] - with_sin[:half]) * scale).astype(bf16)
    return real, imag


def store_both(outs, far, real, imag):
    depth = real.shape[0] // 2
    for i, out in enumerate(outs):
        out[far, 0] = real[i * depth : (i + 1) * depth]
        out[far, 1] = imag[i * depth : (i + 1) * depth]


def opening_kernel(lay, scale, info, place, data, away, keep, cos_ref, sin_ref):
    width = away.shape[-1]
    cores = (1 - place[1], place[1])
    values = jnp.concatenate([data[part, 0, core] for part in range(2) for core in cores], axis=0)
    fill = functools.partial(table_tile, lay, info, place, cos_ref, sin_ref, width=width)
    fill(0, 0)
    for far in range(lay.far):
        spot = slice(far * width, (far + 1) * width)
        store_both((away, keep), far, *turned(values, cos_ref[0, :, spot], sin_ref[0, :, spot], scale))
        if far + 1 < lay.far:
            fill(0, far + 1)
        fill(1, far)


def opening(lay, scale, info, place, data, width):
    depth, rows = data.shape[-2:]
    total = lay.far * width
    half = jax.ShapeDtypeStruct((lay.far, 2, depth, width), bf16)
    return pl.pallas_call(
        functools.partial(opening_kernel, lay, scale),
        out_shape=[half] * 2 + [pltpu.VMEM((2, rows, total), bf16)] * 2,
        grid_spec=pltpu.PrefetchScalarGridSpec(
            num_scalar_prefetch=2,
            grid=(1,),
            in_specs=[pl.BlockSpec((2, 1, 2, depth, rows), lambda t, info, place: (0, 1 - place[0], 0, 0, 0))],
            out_specs=[WHOLE] * 4,
        ),
        compiler_params=pltpu.CompilerParams(vmem_limit_bytes=LIMIT),
        name="opening",
    )(info, place, data)


def closing_kernel(lay, scale, place, data, cos_ref, sin_ref, away, keep):
    width = away.shape[-1]

    def tile(far, carry):
        spot = pl.ds(far * width, width)
        cores = (1 - place[1], place[1])
        values = jnp.concatenate([data[part, place[0], core] for part in range(2) for core in cores], axis=0)
        store_both((away, keep), far, *turned(values, cos_ref[1, :, spot], sin_ref[1, :, spot], scale))
        return carry

    lax.fori_loop(0, lay.far, tile, 0, unroll=True)


def side_kernel(lay, scale, first, other, place, data, cos_ref, sin_ref, out):
    width = out.shape[-1]
    core = 1 - place[1] if other else place[1]
    mine = jnp.where(core == 0, first, 1 - first)
    digit = jnp.where(mine == 1, place[0], 1 - place[0])
    near = 1 - mine

    def tile(far, carry):
        spot = pl.ds(far * width, width)
        values = jnp.concatenate([data[part, digit, core] for part in range(2)], axis=0)
        real, imag = turned(values, cos_ref[near, :, spot], sin_ref[near, :, spot], scale)
        out[far, 0] = real
        out[far, 1] = imag
        return carry

    lax.fori_loop(0, lay.far, tile, 0, unroll=True)


def piece(lay, kernel, count, place, data, tables, width):
    depth = data.shape[-2]
    return pl.pallas_call(
        kernel,
        out_shape=[jax.ShapeDtypeStruct((lay.far, 2, depth, width), bf16)] * count,
        in_specs=[SCALARS] + [WHOLE] * 3,
        out_specs=[WHOLE] * count,
        compiler_params=pltpu.CompilerParams(vmem_limit_bytes=LIMIT),
        name="piece",
    )(place, data, *tables)


def blocks_kernel(lay, place, held, *refs):
    parts = refs[: -lay.far]
    for shift, out in enumerate(refs[-lay.far :]):
        far = lax.rem(place[2] + shift, lay.far)
        out[...] = total_of(held[far], *[part[far] for part in parts]).astype(out.dtype)


def blocks(lay, place, held, *parts):
    shape = held.shape[1:]
    types = [f32] + [bf16] * (lay.far - 1)
    return pl.pallas_call(
        functools.partial(blocks_kernel, lay),
        out_shape=[jax.ShapeDtypeStruct(shape, kind) for kind in types],
        in_specs=[SCALARS] + [WHOLE] * (1 + len(parts)),
        out_specs=[WHOLE] * lay.far,
        compiler_params=pltpu.CompilerParams(vmem_limit_bytes=LIMIT),
        name="blocks",
    )(place, held, *parts)


def fill_left(lay, place, left, own, other):
    width = own.shape[-1]
    for i, source in enumerate((own, other)):
        core = place[1] if i == 0 else 1 - place[1]
        for third in range(lay.far):
            far = lax.rem(place[2] - third + lay.far, lay.far)
            spot = pl.ds(pl.multiple_of(far * width, width), width)
            for part in range(2):
                left[core, part, :, spot] = source[third, part]


def back(values, cos_ref, sin_ref, near, spot):
    contract = (((1,), (1,)), ((), ()))
    with_cos = lax.dot_general(values, cos_ref[near, spot], contract, preferred_element_type=f32)
    with_sin = lax.dot_general(values, sin_ref[near, spot], contract, preferred_element_type=f32)
    half = values.shape[0] // 2
    return with_cos[:half] - with_sin[half:], with_cos[half:] + with_sin[:half]


def rows_of(left, cores):
    values = [left[core, part] for part in range(2) for core in cores]
    return jnp.concatenate(values, axis=0)


def begin_kernel(lay, step, place, own, other, cos_ref, sin_ref, total, left):
    fill_left(lay, place, left, own, other)
    depth = left.shape[2]

    def tile(t, carry):
        spot = pl.ds(t * step, step)
        real, imag = back(rows_of(left, (0, 1)), cos_ref, sin_ref, 1, spot)
        for core in range(2):
            total[core, 0, :, spot] = real[core * depth : (core + 1) * depth]
            total[core, 1, :, spot] = imag[core * depth : (core + 1) * depth]
        return carry

    lax.fori_loop(0, cos_ref.shape[1] // step, tile, 0, unroll=True)


def begin(lay, pair, tables, place):
    _, rows, total = tables[0].shape
    depth = pair[0].shape[-2]
    return pl.pallas_call(
        functools.partial(begin_kernel, lay, tile_of(rows)),
        out_shape=pltpu.VMEM((2, 2, depth, rows), f32),
        in_specs=[SCALARS] + [WHOLE] * 4,
        out_specs=WHOLE,
        scratch_shapes=[pltpu.VMEM((2, 2, depth, total), bf16)],
        compiler_params=pltpu.CompilerParams(vmem_limit_bytes=LIMIT),
        name="begin",
    )(place, *pair, *tables)


def tile_of(rows):
    return 512 if rows % 512 == 0 else rows


def middle_kernel(lay, scale, ending, place, own, other, cos_ref, sin_ref, total, *refs):
    *_, out, begun, left, ready, sent = refs
    fill_left(lay, place, left, own, other)
    slots, *_, step = ready.shape
    copies = []
    for t in range(slots):
        spot = pl.ds(t * step, step)
        real, imag = back(rows_of(left, (ending,)), cos_ref, sin_ref, 0, spot)
        ready[t, 0, 0] = ((total[ending, 0, :, spot] + real) * scale).astype(bf16)
        ready[t, 1, 0] = ((total[ending, 1, :, spot] + imag) * scale).astype(bf16)
        target = out.at[:, place[0], ending : ending + 1, :, spot]
        copies.append(pltpu.make_async_copy(ready.at[t], target, sent.at[t]))
        copies[-1].start()
        real, imag = back(rows_of(left, (1 - ending,)), cos_ref, sin_ref, 1, spot)
        begun[0, :, spot] = real
        begun[1, :, spot] = imag
    for copy in copies:
        copy.wait()


def finish_kernel(lay, scale, place, own, other, cos_ref, sin_ref, *refs):
    *totals, _, out, left, ready, sent = refs
    fill_left(lay, place, left, own, other)
    depth = left.shape[2]
    slots, *_, step = ready.shape
    copies = []
    for t in range(slots):
        spot = pl.ds(t * step, step)
        real, imag = back(rows_of(left, (0, 1)), cos_ref, sin_ref, 0, spot)
        for core, total in enumerate(totals):
            block = slice(core * depth, (core + 1) * depth)
            ready[t, 0, core] = ((total[0, :, spot] + real[block]) * scale).astype(bf16)
            ready[t, 1, core] = ((total[1, :, spot] + imag[block]) * scale).astype(bf16)
        target = out.at[:, 1 - place[0], :, :, spot]
        copies.append(pltpu.make_async_copy(ready.at[t], target, sent.at[t]))
        copies[-1].start()
    for copy in copies:
        copy.wait()


def written(lay, kernel, place, operands, earlier, cores, begun):
    _, rows, cells = operands[2].shape
    depth = operands[0].shape[-2]
    step = tile_of(rows)
    specs = [SCALARS] + [WHOLE] * len(operands)
    if earlier is not None:
        operands = [*operands, earlier]
        specs.append(pl.BlockSpec(memory_space=pl.ANY))
    slots = rows // step
    return pl.pallas_call(
        kernel,
        out_shape=[jax.ShapeDtypeStruct((2, lay.high, 2, depth, rows), bf16)]
        + [pltpu.VMEM((2, depth, rows), f32)] * begun,
        in_specs=specs,
        out_specs=[pl.BlockSpec(memory_space=pl.ANY)] + [WHOLE] * begun,
        scratch_shapes=[
            pltpu.VMEM((2, 2, depth, cells), bf16),
            pltpu.VMEM((slots, 2, cores, depth, step), bf16),
            pltpu.SemaphoreType.DMA((slots,)),
        ],
        input_output_aliases={} if earlier is None else {len(operands): 0},
        compiler_params=pltpu.CompilerParams(vmem_limit_bytes=LIMIT),
    )(place, *operands)


def middle(lay, pair, tables, total, place, ending, scale, earlier=None):
    return written(
        lay, functools.partial(middle_kernel, lay, scale, ending), place, [*pair, *tables, total], earlier, 1, 1
    )


def finish(lay, pair, tables, totals, place, scale, earlier):
    return written(
        lay, functools.partial(finish_kernel, lay, scale), place, [*pair, *tables, *totals], earlier, 2, 0
    )[0]


def in_pieces(lay, facets, offsets, visibilities, weights, mask):
    high, core, far, near = lay.place()
    _, _, _, rows = facets.shape
    _, depth, width = visibilities.shape
    facet_index = lax.axis_index("facet")
    all_rows = rows * lay.strips
    base = lax.axis_index("strip") * rows + facet_index % FROWS * all_rows + NG // 2
    info = jnp.concatenate([jnp.stack([base, core]).astype(jnp.int32), offsets])
    place = jnp.stack([high, core, far, near]).astype(jnp.int32)
    scale = 1.0 / math.sqrt(all_rows)
    data = facets.reshape(2, lay.high, lay.cores, depth, rows)

    def sent(stage, *values):
        return lay.send(values[0] if len(values) == 1 else total_of(*values).astype(bf16), stage, 1)

    def side(first, other):
        return piece(lay, functools.partial(side_kernel, lay, scale, first, other), 1, place, data, tables, width)[0]

    away, keep, *tables = opening(lay, scale, info, place, data, width)
    cross = sent("core", away)
    away = side(0, True)
    first_a = sent("first", keep, cross)
    cross = sent("core", away)
    keep = side(0, False)
    first_b = sent("first", keep, cross)
    away = side(1, True)
    cross = sent("core", away)
    keep = side(1, False)
    second = sent("second", keep, cross, first_a)
    away, keep = piece(lay, functools.partial(closing_kernel, lay, scale), 2, place, data, tables, width)
    cross = sent("core", away)
    own, *others = blocks(lay, place, keep, cross, first_b, second)
    model = total_of(own, *[lay.send(value, "far", 1 + i) for i, value in enumerate(others)])

    factor = weights * mask.astype(f32)
    residual = (factor[None] * (visibilities - model)).astype(bf16)

    def paired(value):
        return [value, sent("core", value)]

    corner = gather_stage(lay, residual, "far", lay.far)
    over_second = sent("second", corner)
    corners = paired(corner)
    total = begin(lay, corners, tables, place)
    over_first = sent("first", corner)
    over_both = sent("first", over_second)
    seconds = paired(over_second)
    update, begun_one = middle(lay, seconds, tables, total, place, 0, scale)
    firsts = paired(over_first)
    update, begun_zero = middle(lay, firsts, tables, total, place, 1, scale, update)
    boths = paired(over_both)
    update = finish(lay, boths, tables, (begun_zero, begun_one), place, scale, update)
    return update.reshape(facets.shape)


def on_device(lay, *arrays):
    if lay.fast:
        return in_pieces(lay, *arrays)
    return in_stages(lay, *arrays)


def solution(mesh):
    placed = (
        P("facet", None, None, "strip"),
        P(),
        P(None, "strip", "facet"),
        P("strip", "facet"),
        P("strip", "facet"),
    )
    lay = Layout(mesh)
    return jax.shard_map(
        functools.partial(on_device, lay),
        mesh=mesh,
        in_specs=placed,
        out_specs=P("facet", None, None, "strip"),
        check_vma=False,
    )
```

```python
import functools
import math

import jax
import jax.numpy as jnp
from jax import lax
from jax.experimental import pallas as pl
from jax.experimental.pallas import tpu as pltpu
from jax.sharding import PartitionSpec as P


NG = 32768
FROWS = 4
FINE = 16
AXES = ("facet", "strip")
bf16 = jnp.bfloat16
f32 = jnp.float32


def unit_circle(count):
    count = count & (NG - 1)
    quarter = (count + NG // 8) >> (NG.bit_length() - 3)
    angle = (count - quarter * (NG // 4)).astype(f32) * (2.0 * math.pi / NG)
    square = angle * angle
    sine = angle * (
        1.0 + square * (-1.0 / 6 + square * (1.0 / 120 + square * (-1.0 / 5040 + square * (1.0 / 362880))))
    )
    cosine = 1.0 + square * (
        -0.5 + square * (1.0 / 24 + square * (-1.0 / 720 + square * (1.0 / 40320 + square * (-1.0 / 3628800))))
    )
    odd = (quarter & 1) == 1
    first = jnp.where(odd, sine, cosine)
    second = jnp.where(odd, cosine, sine)
    return (
        jnp.where(((quarter + 1) & 2) != 0, -first, first),
        jnp.where((quarter & 2) != 0, -second, second),
    )


class Layout:
    def __init__(self, mesh):
        self.strips = mesh.shape["strip"]
        self.facets = mesh.shape["facet"]
        self.cores = 2 if self.strips % 2 == 0 else 1
        self.high = self.strips // self.cores
        self.near = 2 if self.facets % 2 == 0 else 1
        self.far = self.facets // self.near
        self.mixed = self.high == self.near and self.cores == 2
        self.fast = self.mixed and self.high == 2

    def place(self):
        strip = lax.axis_index("strip")
        facet = lax.axis_index("facet")
        return strip // self.cores, strip % self.cores, facet // self.near, facet % self.near

    def permutation(self, move):
        pairs = []
        for facet in range(self.facets):
            for strip in range(self.strips):
                digits = move(strip // self.cores, strip % self.cores, facet // self.near, facet % self.near)
                high, core, far, near = digits
                target = (far * self.near + near) * self.strips + high * self.cores + core
                pairs.append((facet * self.strips + strip, target))
        return pairs

    def along(self, stage, shift):
        def move(high, core, far, near):
            if stage == "core":
                return high, (core + shift) % self.cores, far, near
            if stage == "far":
                return high, core, (far + shift) % self.far, near
            first = "near" if self.mixed and core == 1 else "high"
            second = "high" if first == "near" else "near"
            if (first if stage == "first" else second) == "high":
                return (high + shift) % self.high, core, far, near
            return high, core, far, (near + shift) % self.near

        return self.permutation(move)

    def send(self, value, stage, shift):
        return lax.ppermute(value, AXES, self.along(stage, shift))


def forward_kernel(lay, scale, info, *refs):
    if lay.cores == 2:
        away_in, keep_in, away_out, keep_out, cos_ref, sin_ref = refs
        halves = ((away_in, away_out, 1 - info[1]), (keep_in, keep_out, info[1]))
    else:
        keep_in, keep_out, cos_ref, sin_ref = refs
        halves = ((keep_in, keep_out, info[1]),)
    tile = pl.program_id(0)
    rows, width = cos_ref.shape
    cells = (pl.num_programs(0) * width) // info_offsets(info)
    start = tile * width
    offset = info[2 + start // cells]
    frequency = offset + start % cells + lax.broadcasted_iota(jnp.int32, (1, width), 1)
    coarse_rows = info[0] + FINE * lax.broadcasted_iota(jnp.int32, (rows // FINE, 1), 0)
    fine_rows = lax.broadcasted_iota(jnp.int32, (FINE, 1), 0)
    frequency = frequency & (NG - 1)
    coarse_cos, coarse_sin = unit_circle((coarse_rows & (NG - 1)) * frequency)
    fine_cos, fine_sin = unit_circle(fine_rows * frequency)
    for block in range(rows // FINE):
        c = coarse_cos[block : block + 1]
        s = coarse_sin[block : block + 1]
        cos_ref[block * FINE : (block + 1) * FINE] = (c * fine_cos - s * fine_sin).astype(bf16)
        sin_ref[block * FINE : (block + 1) * FINE] = (s * fine_cos + c * fine_sin).astype(bf16)
    near = lax.rem(tile, lay.near)
    for data, out, core in halves:
        high, depth = data.shape[1], data.shape[-2]
        values = data[...].reshape(2 * high * depth, rows)
        with_cos = jnp.dot(values, cos_ref[...], preferred_element_type=f32).reshape(2, high, depth, width)
        with_sin = jnp.dot(values, sin_ref[...], preferred_element_type=f32).reshape(2, high, depth, width)
        real = ((with_cos[0] + with_sin[1]) * scale).astype(bf16)
        imag = ((with_cos[1] - with_sin[0]) * scale).astype(bf16)
        for h in range(high):
            spot = h * lay.near + near
            if lay.mixed:
                spot = jnp.where(core == 1, near * lay.high + h, spot)
            out[spot, 0, 0] = real[h]
            out[spot, 0, 1] = imag[h]


def info_offsets(info):
    return info.shape[0] - 2


def forward(lay, data, info, chunk, chunks, width, scale):
    rows = data.shape[-1]
    depth = data.shape[3] // chunks
    tiles = lay.facets
    half = (2, lay.high, None, depth, rows)
    out_block = (lay.high * lay.near, 1, 2, depth, width)
    out_shape = jax.ShapeDtypeStruct((lay.high * lay.near, lay.far, 2, depth, width), bf16)
    out_spec = pl.BlockSpec(out_block, lambda t, info: (0, t // lay.near, 0, 0, 0))
    table_shape = jax.ShapeDtypeStruct((rows, tiles * width), bf16)
    table_spec = pl.BlockSpec((rows, width), lambda t, info: (0, t))
    in_specs = [pl.BlockSpec(half, lambda t, info: (0, 0, info[1], chunk, 0))]
    if lay.cores == 2:
        in_specs.insert(0, pl.BlockSpec(half, lambda t, info: (0, 0, 1 - info[1], chunk, 0)))
    n = len(in_specs)
    return pl.pallas_call(
        functools.partial(forward_kernel, lay, scale),
        out_shape=(out_shape,) * n + (table_shape,) * 2,
        grid_spec=pltpu.PrefetchScalarGridSpec(
            num_scalar_prefetch=1,
            grid=(tiles,),
            in_specs=in_specs,
            out_specs=(out_spec,) * n + (table_spec,) * 2,
        ),
        compiler_params=pltpu.CompilerParams(vmem_limit_bytes=58 << 20),
        name="forward",
    )(info, *([data] * n))


def adjoint_kernel(lay, scale, place, *refs):
    sources = refs[: lay.cores]
    cos_ref, sin_ref, out_ref, left = refs[lay.cores :]
    width = sources[0].shape[-1]
    depth = sources[0].shape[-2]

    @pl.when(pl.program_id(0) == 0)
    def _():
        for i, source in enumerate(sources):
            core = place[1] if i == 0 else 1 - place[1]
            for first in range(source.shape[0]):
                for second in range(source.shape[1]):
                    shifts = (first, second)
                    high = lax.rem(place[0] - shifts[0] + lay.high, lay.high)
                    near = lax.rem(place[3] - shifts[1] + lay.near, lay.near)
                    if lay.mixed:
                        high = jnp.where(core == 1, lax.rem(place[0] - second + lay.high, lay.high), high)
                        near = jnp.where(core == 1, lax.rem(place[3] - first + lay.near, lay.near), near)
                    for third in range(lay.far):
                        far = lax.rem(place[2] - third + lay.far, lay.far)
                        spot = pl.multiple_of((far * lay.near + near) * width, width)
                        for part in range(2):
                            left[i, part, high, :, pl.ds(spot, width)] = source[first, second, third, part]

    for i in range(len(sources)):
        core = place[1] if i == 0 else 1 - place[1]
        values = left[i].reshape(2 * lay.high * depth, left.shape[-1])
        contract = (((1,), (1,)), ((), ()))
        with_cos = lax.dot_general(values, cos_ref[...], contract, preferred_element_type=f32)
        with_sin = lax.dot_general(values, sin_ref[...], contract, preferred_element_type=f32)
        shape = (2, lay.high, depth, with_cos.shape[-1])
        with_cos, with_sin = with_cos.reshape(shape), with_sin.reshape(shape)
        real = ((with_cos[0] - with_sin[1]) * scale).astype(bf16)
        imag = ((with_cos[1] + with_sin[0]) * scale).astype(bf16)
        for h in range(lay.high):
            out_ref[0, h, core] = real[h]
            out_ref[1, h, core] = imag[h]


def adjoint(lay, sources, cos_table, sin_table, place, shape, chunk, chunks, scale):
    rows, total = cos_table.shape
    depth = shape[3] // chunks
    tile = 256 if rows % 256 == 0 else rows
    source_spec = pl.BlockSpec(sources[0].shape, lambda t, place: (0,) * 6)
    table_spec = pl.BlockSpec((tile, total), lambda t, place: (t, 0))
    return pl.pallas_call(
        functools.partial(adjoint_kernel, lay, scale),
        out_shape=jax.ShapeDtypeStruct(shape, bf16),
        grid_spec=pltpu.PrefetchScalarGridSpec(
            num_scalar_prefetch=1,
            grid=(rows // tile,),
            in_specs=[source_spec] * len(sources) + [table_spec] * 2,
            out_specs=pl.BlockSpec((2, lay.high, lay.cores, depth, tile), lambda t, place: (0, 0, 0, chunk, t)),
            scratch_shapes=[pltpu.VMEM((len(sources), 2, lay.high, depth, total), bf16)],
        ),
        compiler_params=pltpu.CompilerParams(vmem_limit_bytes=58 << 20),
        name="adjoint",
    )(place, *sources, cos_table, sin_table)


def pick(value, index):
    return lax.dynamic_index_in_dim(value, index, 0, keepdims=False)


def total_of(*values):
    return functools.reduce(jnp.add, [v.astype(f32) for v in values])


def scatter_stage(lay, value, stage, size, mine):
    received = [
        lay.send(pick(value, lax.rem(mine + shift, size)), stage, shift) for shift in range(1, size)
    ]
    return total_of(pick(value, mine), *received)


def gather_stage(lay, value, stage, size):
    return jnp.stack([value] + [lay.send(value, stage, shift) for shift in range(1, size)])


def in_stages(lay, facets, offsets, visibilities, weights, mask):
    high, core, far, near = lay.place()
    _, _, _, rows = facets.shape
    width = visibilities.shape[2]
    own_columns = visibilities.shape[1]
    facet_index = lax.axis_index("facet")
    all_rows = rows * lay.strips
    base = lax.axis_index("strip") * rows + facet_index % FROWS * all_rows + NG // 2
    info = jnp.concatenate([jnp.stack([base, core]).astype(jnp.int32), offsets])
    place = jnp.stack([high, core, far, near]).astype(jnp.int32)
    scale = 1.0 / math.sqrt(all_rows)
    data = facets.reshape(2, lay.high, lay.cores, own_columns, rows)
    *partial, cos_table, sin_table = forward(lay, data, info, 0, 1, width, scale)
    value = partial[-1]
    if lay.cores == 2:
        value = total_of(value, lay.send(partial[0], "core", 1)).astype(bf16)
    sizes = (lay.high, lay.near)
    digits = (high, near)
    if lay.mixed:
        digits = (jnp.where(core == 1, near, high), jnp.where(core == 1, high, near))
    value = value.reshape(*sizes, *value.shape[1:])
    value = scatter_stage(lay, value, "first", sizes[0], digits[0]).astype(bf16)
    value = scatter_stage(lay, value, "second", sizes[1], digits[1]).astype(bf16)
    model = scatter_stage(lay, value, "far", lay.far, far)
    factor = weights * mask.astype(f32)
    residual = (factor[None] * (visibilities - model)).astype(bf16)
    value = gather_stage(lay, residual, "far", lay.far)
    value = gather_stage(lay, value, "second", sizes[1])
    value = gather_stage(lay, value, "first", sizes[0])
    sources = [value]
    if lay.cores == 2:
        sources.append(lay.send(value, "core", 1))
    update = adjoint(lay, sources, cos_table, sin_table, place, data.shape, 0, 1, scale)
    return update.reshape(facets.shape)


WHOLE = pl.BlockSpec(memory_space=pltpu.VMEM)
SCALARS = pl.BlockSpec(memory_space=pltpu.SMEM)


def table_tile(lay, info, place, cos_ref, sin_ref, near, far, width):
    rows = cos_ref.shape[1]
    cells = lay.facets * width // info_offsets(info)
    digit = place[3] if near == 1 else 1 - place[3]
    blocks = rows // FINE
    middle = blocks // 2
    start = (far * lay.near + digit) * width
    frequency = info[2 + start // cells] + start % cells + lax.broadcasted_iota(jnp.int32, (1, width), 1)
    frequency = frequency & (NG - 1)
    middle_rows = info[0] + FINE * middle + lax.broadcasted_iota(jnp.int32, (FINE, 1), 0)
    cos_mid, sin_mid = unit_circle((middle_rows & (NG - 1)) * frequency)
    steps = -(-(middle + 1) // 8) * 8
    cos_step, sin_step = unit_circle(FINE * lax.broadcasted_iota(jnp.int32, (steps, 1), 0) * frequency)
    spot = slice(far * width, (far + 1) * width)

    def write(block, cosine, sine):
        if 0 <= block < blocks:
            cos_ref[near, block * FINE : (block + 1) * FINE, spot] = cosine.astype(bf16)
            sin_ref[near, block * FINE : (block + 1) * FINE, spot] = sine.astype(bf16)

    write(middle, cos_mid, sin_mid)
    for away in range(1, middle + 1):
        c = cos_step[away : away + 1]
        s = sin_step[away : away + 1]
        cc, ss, sc, cs = cos_mid * c, sin_mid * s, sin_mid * c, cos_mid * s
        write(middle + away, cc - ss, sc + cs)
        write(middle - away, cc + ss, sc - cs)


LIMIT = 8 << 20
OPENING_LIMIT = 12 << 20


def turned(values, cosine, sine, scale):
    half = values.shape[0] // 2
    with_cos = jnp.dot(values, cosine, preferred_element_type=f32)
    with_sin = jnp.dot(values, sine, preferred_element_type=f32)
    real = ((with_cos[:half] + with_sin[half:]) * scale).astype(bf16)
    imag = ((with_cos[half:] - with_sin[:half]) * scale).astype(bf16)
    return real, imag


def store_both(outs, far, real, imag):
    depth = real.shape[0] // 2
    for i, out in enumerate(outs):
        out[far, 0] = real[i * depth : (i + 1) * depth]
        out[far, 1] = imag[i * depth : (i + 1) * depth]


def opening_kernel(lay, scale, info, place, data, away, keep, cos_ref, sin_ref):
    width = away.shape[-1]
    cores = (1 - place[1], place[1])
    values = jnp.concatenate([data[part, 0, core] for part in range(2) for core in cores], axis=0)
    fill = functools.partial(table_tile, lay, info, place, cos_ref, sin_ref, width=width)
    fill(0, 0)
    for far in range(lay.far):
        spot = slice(far * width, (far + 1) * width)
        store_both((away, keep), far, *turned(values, cos_ref[0, :, spot], sin_ref[0, :, spot], scale))
        if far + 1 < lay.far:
            fill(0, far + 1)
        fill(1, far)


def opening(lay, scale, info, place, data, width):
    depth, rows = data.shape[-2:]
    total = lay.far * width
    half = jax.ShapeDtypeStruct((lay.far, 2, depth, width), bf16)
    return pl.pallas_call(
        functools.partial(opening_kernel, lay, scale),
        out_shape=[half] * 2 + [pltpu.VMEM((2, rows, total), bf16)] * 2,
        grid_spec=pltpu.PrefetchScalarGridSpec(
            num_scalar_prefetch=2,
            grid=(1,),
            in_specs=[pl.BlockSpec((2, 1, 2, depth, rows), lambda t, info, place: (0, 1 - place[0], 0, 0, 0))],
            out_specs=[WHOLE] * 4,
        ),
        compiler_params=pltpu.CompilerParams(vmem_limit_bytes=OPENING_LIMIT),
        name="opening",
    )(info, place, data)


def closing_kernel(lay, scale, place, data, cos_ref, sin_ref, away, keep):
    width = away.shape[-1]

    def tile(far, carry):
        spot = pl.ds(far * width, width)
        cores = (1 - place[1], place[1])
        values = jnp.concatenate([data[part, place[0], core] for part in range(2) for core in cores], axis=0)
        store_both((away, keep), far, *turned(values, cos_ref[1, :, spot], sin_ref[1, :, spot], scale))
        return carry

    lax.fori_loop(0, lay.far, tile, 0, unroll=True)


def side_kernel(lay, scale, first, other, place, data, cos_ref, sin_ref, out):
    width = out.shape[-1]
    core = 1 - place[1] if other else place[1]
    mine = jnp.where(core == 0, first, 1 - first)
    digit = jnp.where(mine == 1, place[0], 1 - place[0])
    near = 1 - mine

    def tile(far, carry):
        spot = pl.ds(far * width, width)
        values = jnp.concatenate([data[part, digit, core] for part in range(2)], axis=0)
        real, imag = turned(values, cos_ref[near, :, spot], sin_ref[near, :, spot], scale)
        out[far, 0] = real
        out[far, 1] = imag
        return carry

    lax.fori_loop(0, lay.far, tile, 0, unroll=True)


def piece(lay, kernel, count, place, data, tables, width):
    depth = data.shape[-2]
    return pl.pallas_call(
        kernel,
        out_shape=[jax.ShapeDtypeStruct((lay.far, 2, depth, width), bf16)] * count,
        in_specs=[SCALARS] + [WHOLE] * 3,
        out_specs=[WHOLE] * count,
        compiler_params=pltpu.CompilerParams(vmem_limit_bytes=LIMIT),
        name="piece",
    )(place, data, *tables)


def blocks_kernel(lay, place, held, *refs):
    parts = refs[: -lay.far]
    for shift, out in enumerate(refs[-lay.far :]):
        far = lax.rem(place[2] + shift, lay.far)
        out[...] = total_of(held[far], *[part[far] for part in parts]).astype(out.dtype)


def blocks(lay, place, held, *parts):
    shape = held.shape[1:]
    types = [f32] + [bf16] * (lay.far - 1)
    return pl.pallas_call(
        functools.partial(blocks_kernel, lay),
        out_shape=[jax.ShapeDtypeStruct(shape, kind) for kind in types],
        in_specs=[SCALARS] + [WHOLE] * (1 + len(parts)),
        out_specs=[WHOLE] * lay.far,
        compiler_params=pltpu.CompilerParams(vmem_limit_bytes=LIMIT),
        name="blocks",
    )(place, held, *parts)


def fill_left(lay, place, left, own, other):
    width = own.shape[-1]
    for i, source in enumerate((own, other)):
        core = place[1] if i == 0 else 1 - place[1]
        for third in range(lay.far):
            far = lax.rem(place[2] - third + lay.far, lay.far)
            spot = pl.ds(pl.multiple_of(far * width, width), width)
            for part in range(2):
                left[core, part, :, spot] = source[third, part]


def back(values, cos_ref, sin_ref, near, spot):
    contract = (((1,), (1,)), ((), ()))
    with_cos = lax.dot_general(values, cos_ref[near, spot], contract, preferred_element_type=f32)
    with_sin = lax.dot_general(values, sin_ref[near, spot], contract, preferred_element_type=f32)
    half = values.shape[0] // 2
    return with_cos[:half] - with_sin[half:], with_cos[half:] + with_sin[:half]


def rows_of(left, cores):
    values = [left[core, part] for part in range(2) for core in cores]
    return jnp.concatenate(values, axis=0)


def begin_kernel(lay, step, place, own, other, cos_ref, sin_ref, total, left):
    fill_left(lay, place, left, own, other)
    depth = left.shape[2]

    def tile(t, carry):
        spot = pl.ds(t * step, step)
        real, imag = back(rows_of(left, (0, 1)), cos_ref, sin_ref, 1, spot)
        for core in range(2):
            total[core, 0, :, spot] = real[core * depth : (core + 1) * depth]
            total[core, 1, :, spot] = imag[core * depth : (core + 1) * depth]
        return carry

    lax.fori_loop(0, cos_ref.shape[1] // step, tile, 0, unroll=True)


def begin(lay, pair, tables, place):
    _, rows, total = tables[0].shape
    depth = pair[0].shape[-2]
    return pl.pallas_call(
        functools.partial(begin_kernel, lay, tile_of(rows)),
        out_shape=pltpu.VMEM((2, 2, depth, rows), f32),
        in_specs=[SCALARS] + [WHOLE] * 4,
        out_specs=WHOLE,
        scratch_shapes=[pltpu.VMEM((2, 2, depth, total), bf16)],
        compiler_params=pltpu.CompilerParams(vmem_limit_bytes=LIMIT),
        name="begin",
    )(place, *pair, *tables)


def tile_of(rows):
    return 512 if rows % 512 == 0 else rows


def middle_kernel(lay, scale, ending, place, own, other, cos_ref, sin_ref, total, *refs):
    *_, out, begun, left, ready, sent = refs
    fill_left(lay, place, left, own, other)
    slots, *_, step = ready.shape
    copies = []
    for t in range(slots):
        spot = pl.ds(t * step, step)
        real, imag = back(rows_of(left, (ending,)), cos_ref, sin_ref, 0, spot)
        ready[t, 0, 0] = ((total[ending, 0, :, spot] + real) * scale).astype(bf16)
        ready[t, 1, 0] = ((total[ending, 1, :, spot] + imag) * scale).astype(bf16)
        target = out.at[:, place[0], ending : ending + 1, :, spot]
        copies.append(pltpu.make_async_copy(ready.at[t], target, sent.at[t]))
        copies[-1].start()
        real, imag = back(rows_of(left, (1 - ending,)), cos_ref, sin_ref, 1, spot)
        begun[0, :, spot] = real
        begun[1, :, spot] = imag
    for copy in copies:
        copy.wait()


def finish_kernel(lay, scale, place, own, other, cos_ref, sin_ref, *refs):
    *totals, _, out, left, ready, sent = refs
    fill_left(lay, place, left, own, other)
    depth = left.shape[2]
    slots, *_, step = ready.shape
    copies = []
    for t in range(slots):
        spot = pl.ds(t * step, step)
        real, imag = back(rows_of(left, (0, 1)), cos_ref, sin_ref, 0, spot)
        for core, total in enumerate(totals):
            block = slice(core * depth, (core + 1) * depth)
            ready[t, 0, core] = ((total[0, :, spot] + real[block]) * scale).astype(bf16)
            ready[t, 1, core] = ((total[1, :, spot] + imag[block]) * scale).astype(bf16)
        target = out.at[:, 1 - place[0], :, :, spot]
        copies.append(pltpu.make_async_copy(ready.at[t], target, sent.at[t]))
        copies[-1].start()
    for copy in copies:
        copy.wait()


OUT_SLOTS = 2


def written(lay, kernel, place, operands, earlier, cores, begun):
    _, rows, cells = operands[2].shape
    depth = operands[0].shape[-2]
    step = rows // OUT_SLOTS if rows % (OUT_SLOTS * 128) == 0 else rows
    specs = [SCALARS] + [WHOLE] * len(operands)
    if earlier is not None:
        operands = [*operands, earlier]
        specs.append(pl.BlockSpec(memory_space=pl.ANY))
    slots = rows // step
    return pl.pallas_call(
        kernel,
        out_shape=[jax.ShapeDtypeStruct((2, lay.high, 2, depth, rows), bf16)]
        + [pltpu.VMEM((2, depth, rows), f32)] * begun,
        in_specs=specs,
        out_specs=[pl.BlockSpec(memory_space=pl.ANY)] + [WHOLE] * begun,
        scratch_shapes=[
            pltpu.VMEM((2, 2, depth, cells), bf16),
            pltpu.VMEM((slots, 2, cores, depth, step), bf16),
            pltpu.SemaphoreType.DMA((slots,)),
        ],
        input_output_aliases={} if earlier is None else {len(operands): 0},
        compiler_params=pltpu.CompilerParams(vmem_limit_bytes=LIMIT),
    )(place, *operands)


def middle(lay, pair, tables, total, place, ending, scale, earlier=None):
    return written(
        lay, functools.partial(middle_kernel, lay, scale, ending), place, [*pair, *tables, total], earlier, 1, 1
    )


def finish(lay, pair, tables, totals, place, scale, earlier):
    return written(
        lay, functools.partial(finish_kernel, lay, scale), place, [*pair, *tables, *totals], earlier, 2, 0
    )[0]


def in_pieces(lay, facets, offsets, visibilities, weights, mask):
    high, core, far, near = lay.place()
    _, _, _, rows = facets.shape
    _, depth, width = visibilities.shape
    facet_index = lax.axis_index("facet")
    all_rows = rows * lay.strips
    base = lax.axis_index("strip") * rows + facet_index % FROWS * all_rows + NG // 2
    info = jnp.concatenate([jnp.stack([base, core]).astype(jnp.int32), offsets])
    place = jnp.stack([high, core, far, near]).astype(jnp.int32)
    scale = 1.0 / math.sqrt(all_rows)
    data = facets.reshape(2, lay.high, lay.cores, depth, rows)

    def sent(stage, *values):
        return lay.send(values[0] if len(values) == 1 else total_of(*values).astype(bf16), stage, 1)

    def side(first, other):
        return piece(lay, functools.partial(side_kernel, lay, scale, first, other), 1, place, data, tables, width)[0]

    away, keep, *tables = opening(lay, scale, info, place, data, width)
    cross = sent("core", away)
    away = side(0, True)
    first_a = sent("first", keep, cross)
    cross = sent("core", away)
    keep = side(0, False)
    first_b = sent("first", keep, cross)
    away = side(1, True)
    cross = sent("core", away)
    keep = side(1, False)
    second = sent("second", keep, cross, first_a)
    away, keep = piece(lay, functools.partial(closing_kernel, lay, scale), 2, place, data, tables, width)
    cross = sent("core", away)
    own, *others = blocks(lay, place, keep, cross, first_b, second)
    model = total_of(own, *[lay.send(value, "far", 1 + i) for i, value in enumerate(others)])

    factor = weights * mask.astype(f32)
    residual = (factor[None] * (visibilities - model)).astype(bf16)

    def paired(value):
        return [value, sent("core", value)]

    corner = gather_stage(lay, residual, "far", lay.far)
    over_second = sent("second", corner)
    corners = paired(corner)
    total = begin(lay, corners, tables, place)
    over_first = sent("first", corner)
    over_both = sent("first", over_second)
    seconds = paired(over_second)
    update, begun_one = middle(lay, seconds, tables, total, place, 0, scale)
    firsts = paired(over_first)
    update, begun_zero = middle(lay, firsts, tables, total, place, 1, scale, update)
    boths = paired(over_both)
    update = finish(lay, boths, tables, (begun_zero, begun_one), place, scale, update)
    return update.reshape(facets.shape)


def on_device(lay, *arrays):
    if lay.fast:
        return in_pieces(lay, *arrays)
    return in_stages(lay, *arrays)


def solution(mesh):
    placed = (
        P("facet", None, None, "strip"),
        P(),
        P(None, "strip", "facet"),
        P("strip", "facet"),
        P("strip", "facet"),
    )
    lay = Layout(mesh)
    return jax.shard_map(
        functools.partial(on_device, lay),
        mesh=mesh,
        in_specs=placed,
        out_specs=P("facet", None, None, "strip"),
        check_vma=False,
    )
```

```python
import functools
import math

import jax
import jax.numpy as jnp
from jax import lax
from jax.experimental import pallas as pl
from jax.experimental.pallas import tpu as pltpu
from jax.sharding import PartitionSpec as P


NG = 32768
FROWS = 4
FINE = 16
AXES = ("facet", "strip")
bf16 = jnp.bfloat16
f32 = jnp.float32


def unit_circle(count):
    count = count & (NG - 1)
    quarter = (count + NG // 8) >> (NG.bit_length() - 3)
    angle = (count - quarter * (NG // 4)).astype(f32) * (2.0 * math.pi / NG)
    square = angle * angle
    sine = angle * (
        1.0 + square * (-1.0 / 6 + square * (1.0 / 120 + square * (-1.0 / 5040 + square * (1.0 / 362880))))
    )
    cosine = 1.0 + square * (
        -0.5 + square * (1.0 / 24 + square * (-1.0 / 720 + square * (1.0 / 40320 + square * (-1.0 / 3628800))))
    )
    odd = (quarter & 1) == 1
    first = jnp.where(odd, sine, cosine)
    second = jnp.where(odd, cosine, sine)
    return (
        jnp.where(((quarter + 1) & 2) != 0, -first, first),
        jnp.where((quarter & 2) != 0, -second, second),
    )


class Layout:
    def __init__(self, mesh):
        self.strips = mesh.shape["strip"]
        self.facets = mesh.shape["facet"]
        self.cores = 2 if self.strips % 2 == 0 else 1
        self.high = self.strips // self.cores
        self.near = 2 if self.facets % 2 == 0 else 1
        self.far = self.facets // self.near
        self.mixed = self.high == self.near and self.cores == 2
        self.fast = self.mixed and self.high == 2

    def place(self):
        strip = lax.axis_index("strip")
        facet = lax.axis_index("facet")
        return strip // self.cores, strip % self.cores, facet // self.near, facet % self.near

    def permutation(self, move):
        pairs = []
        for facet in range(self.facets):
            for strip in range(self.strips):
                digits = move(strip // self.cores, strip % self.cores, facet // self.near, facet % self.near)
                high, core, far, near = digits
                target = (far * self.near + near) * self.strips + high * self.cores + core
                pairs.append((facet * self.strips + strip, target))
        return pairs

    def along(self, stage, shift):
        def move(high, core, far, near):
            if stage == "core":
                return high, (core + shift) % self.cores, far, near
            if stage == "far":
                return high, core, (far + shift) % self.far, near
            first = "near" if self.mixed and core == 1 else "high"
            second = "high" if first == "near" else "near"
            if (first if stage == "first" else second) == "high":
                return (high + shift) % self.high, core, far, near
            return high, core, far, (near + shift) % self.near

        return self.permutation(move)

    def send(self, value, stage, shift):
        return lax.ppermute(value, AXES, self.along(stage, shift))


def forward_kernel(lay, scale, info, *refs):
    if lay.cores == 2:
        away_in, keep_in, away_out, keep_out, cos_ref, sin_ref = refs
        halves = ((away_in, away_out, 1 - info[1]), (keep_in, keep_out, info[1]))
    else:
        keep_in, keep_out, cos_ref, sin_ref = refs
        halves = ((keep_in, keep_out, info[1]),)
    tile = pl.program_id(0)
    rows, width = cos_ref.shape
    cells = (pl.num_programs(0) * width) // info_offsets(info)
    start = tile * width
    offset = info[2 + start // cells]
    frequency = offset + start % cells + lax.broadcasted_iota(jnp.int32, (1, width), 1)
    coarse_rows = info[0] + FINE * lax.broadcasted_iota(jnp.int32, (rows // FINE, 1), 0)
    fine_rows = lax.broadcasted_iota(jnp.int32, (FINE, 1), 0)
    frequency = frequency & (NG - 1)
    coarse_cos, coarse_sin = unit_circle((coarse_rows & (NG - 1)) * frequency)
    fine_cos, fine_sin = unit_circle(fine_rows * frequency)
    for block in range(rows // FINE):
        c = coarse_cos[block : block + 1]
        s = coarse_sin[block : block + 1]
        cos_ref[block * FINE : (block + 1) * FINE] = (c * fine_cos - s * fine_sin).astype(bf16)
        sin_ref[block * FINE : (block + 1) * FINE] = (s * fine_cos + c * fine_sin).astype(bf16)
    near = lax.rem(tile, lay.near)
    for data, out, core in halves:
        high, depth = data.shape[1], data.shape[-2]
        values = data[...].reshape(2 * high * depth, rows)
        with_cos = jnp.dot(values, cos_ref[...], preferred_element_type=f32).reshape(2, high, depth, width)
        with_sin = jnp.dot(values, sin_ref[...], preferred_element_type=f32).reshape(2, high, depth, width)
        real = ((with_cos[0] + with_sin[1]) * scale).astype(bf16)
        imag = ((with_cos[1] - with_sin[0]) * scale).astype(bf16)
        for h in range(high):
            spot = h * lay.near + near
            if lay.mixed:
                spot = jnp.where(core == 1, near * lay.high + h, spot)
            out[spot, 0, 0] = real[h]
            out[spot, 0, 1] = imag[h]


def info_offsets(info):
    return info.shape[0] - 2


def forward(lay, data, info, chunk, chunks, width, scale):
    rows = data.shape[-1]
    depth = data.shape[3] // chunks
    tiles = lay.facets
    half = (2, lay.high, None, depth, rows)
    out_block = (lay.high * lay.near, 1, 2, depth, width)
    out_shape = jax.ShapeDtypeStruct((lay.high * lay.near, lay.far, 2, depth, width), bf16)
    out_spec = pl.BlockSpec(out_block, lambda t, info: (0, t // lay.near, 0, 0, 0))
    table_shape = jax.ShapeDtypeStruct((rows, tiles * width), bf16)
    table_spec = pl.BlockSpec((rows, width), lambda t, info: (0, t))
    in_specs = [pl.BlockSpec(half, lambda t, info: (0, 0, info[1], chunk, 0))]
    if lay.cores == 2:
        in_specs.insert(0, pl.BlockSpec(half, lambda t, info: (0, 0, 1 - info[1], chunk, 0)))
    n = len(in_specs)
    return pl.pallas_call(
        functools.partial(forward_kernel, lay, scale),
        out_shape=(out_shape,) * n + (table_shape,) * 2,
        grid_spec=pltpu.PrefetchScalarGridSpec(
            num_scalar_prefetch=1,
            grid=(tiles,),
            in_specs=in_specs,
            out_specs=(out_spec,) * n + (table_spec,) * 2,
        ),
        compiler_params=pltpu.CompilerParams(vmem_limit_bytes=58 << 20),
        name="forward",
    )(info, *([data] * n))


def adjoint_kernel(lay, scale, place, *refs):
    sources = refs[: lay.cores]
    cos_ref, sin_ref, out_ref, left = refs[lay.cores :]
    width = sources[0].shape[-1]
    depth = sources[0].shape[-2]

    @pl.when(pl.program_id(0) == 0)
    def _():
        for i, source in enumerate(sources):
            core = place[1] if i == 0 else 1 - place[1]
            for first in range(source.shape[0]):
                for second in range(source.shape[1]):
                    shifts = (first, second)
                    high = lax.rem(place[0] - shifts[0] + lay.high, lay.high)
                    near = lax.rem(place[3] - shifts[1] + lay.near, lay.near)
                    if lay.mixed:
                        high = jnp.where(core == 1, lax.rem(place[0] - second + lay.high, lay.high), high)
                        near = jnp.where(core == 1, lax.rem(place[3] - first + lay.near, lay.near), near)
                    for third in range(lay.far):
                        far = lax.rem(place[2] - third + lay.far, lay.far)
                        spot = pl.multiple_of((far * lay.near + near) * width, width)
                        for part in range(2):
                            left[i, part, high, :, pl.ds(spot, width)] = source[first, second, third, part]

    for i in range(len(sources)):
        core = place[1] if i == 0 else 1 - place[1]
        values = left[i].reshape(2 * lay.high * depth, left.shape[-1])
        contract = (((1,), (1,)), ((), ()))
        with_cos = lax.dot_general(values, cos_ref[...], contract, preferred_element_type=f32)
        with_sin = lax.dot_general(values, sin_ref[...], contract, preferred_element_type=f32)
        shape = (2, lay.high, depth, with_cos.shape[-1])
        with_cos, with_sin = with_cos.reshape(shape), with_sin.reshape(shape)
        real = ((with_cos[0] - with_sin[1]) * scale).astype(bf16)
        imag = ((with_cos[1] + with_sin[0]) * scale).astype(bf16)
        for h in range(lay.high):
            out_ref[0, h, core] = real[h]
            out_ref[1, h, core] = imag[h]


def adjoint(lay, sources, cos_table, sin_table, place, shape, chunk, chunks, scale):
    rows, total = cos_table.shape
    depth = shape[3] // chunks
    tile = 256 if rows % 256 == 0 else rows
    source_spec = pl.BlockSpec(sources[0].shape, lambda t, place: (0,) * 6)
    table_spec = pl.BlockSpec((tile, total), lambda t, place: (t, 0))
    return pl.pallas_call(
        functools.partial(adjoint_kernel, lay, scale),
        out_shape=jax.ShapeDtypeStruct(shape, bf16),
        grid_spec=pltpu.PrefetchScalarGridSpec(
            num_scalar_prefetch=1,
            grid=(rows // tile,),
            in_specs=[source_spec] * len(sources) + [table_spec] * 2,
            out_specs=pl.BlockSpec((2, lay.high, lay.cores, depth, tile), lambda t, place: (0, 0, 0, chunk, t)),
            scratch_shapes=[pltpu.VMEM((len(sources), 2, lay.high, depth, total), bf16)],
        ),
        compiler_params=pltpu.CompilerParams(vmem_limit_bytes=58 << 20),
        name="adjoint",
    )(place, *sources, cos_table, sin_table)


def pick(value, index):
    return lax.dynamic_index_in_dim(value, index, 0, keepdims=False)


def total_of(*values):
    return functools.reduce(jnp.add, [v.astype(f32) for v in values])


def scatter_stage(lay, value, stage, size, mine):
    received = [
        lay.send(pick(value, lax.rem(mine + shift, size)), stage, shift) for shift in range(1, size)
    ]
    return total_of(pick(value, mine), *received)


def gather_stage(lay, value, stage, size):
    return jnp.stack([value] + [lay.send(value, stage, shift) for shift in range(1, size)])


def in_stages(lay, facets, offsets, visibilities, weights, mask):
    high, core, far, near = lay.place()
    _, _, _, rows = facets.shape
    width = visibilities.shape[2]
    own_columns = visibilities.shape[1]
    facet_index = lax.axis_index("facet")
    all_rows = rows * lay.strips
    base = lax.axis_index("strip") * rows + facet_index % FROWS * all_rows + NG // 2
    info = jnp.concatenate([jnp.stack([base, core]).astype(jnp.int32), offsets])
    place = jnp.stack([high, core, far, near]).astype(jnp.int32)
    scale = 1.0 / math.sqrt(all_rows)
    data = facets.reshape(2, lay.high, lay.cores, own_columns, rows)
    *partial, cos_table, sin_table = forward(lay, data, info, 0, 1, width, scale)
    value = partial[-1]
    if lay.cores == 2:
        value = total_of(value, lay.send(partial[0], "core", 1)).astype(bf16)
    sizes = (lay.high, lay.near)
    digits = (high, near)
    if lay.mixed:
        digits = (jnp.where(core == 1, near, high), jnp.where(core == 1, high, near))
    value = value.reshape(*sizes, *value.shape[1:])
    value = scatter_stage(lay, value, "first", sizes[0], digits[0]).astype(bf16)
    value = scatter_stage(lay, value, "second", sizes[1], digits[1]).astype(bf16)
    model = scatter_stage(lay, value, "far", lay.far, far)
    factor = weights * mask.astype(f32)
    residual = (factor[None] * (visibilities - model)).astype(bf16)
    value = gather_stage(lay, residual, "far", lay.far)
    value = gather_stage(lay, value, "second", sizes[1])
    value = gather_stage(lay, value, "first", sizes[0])
    sources = [value]
    if lay.cores == 2:
        sources.append(lay.send(value, "core", 1))
    update = adjoint(lay, sources, cos_table, sin_table, place, data.shape, 0, 1, scale)
    return update.reshape(facets.shape)


WHOLE = pl.BlockSpec(memory_space=pltpu.VMEM)
SCALARS = pl.BlockSpec(memory_space=pltpu.SMEM)


def table_tile(lay, info, place, cos_ref, sin_ref, near, far, width):
    rows = cos_ref.shape[1]
    cells = lay.facets * width // info_offsets(info)
    digit = place[3] if near == 1 else 1 - place[3]
    blocks = rows // FINE
    middle = blocks // 2
    start = (far * lay.near + digit) * width
    frequency = info[2 + start // cells] + start % cells + lax.broadcasted_iota(jnp.int32, (1, width), 1)
    frequency = frequency & (NG - 1)
    middle_rows = info[0] + FINE * middle + lax.broadcasted_iota(jnp.int32, (FINE, 1), 0)
    cos_mid, sin_mid = unit_circle((middle_rows & (NG - 1)) * frequency)
    steps = -(-(middle + 1) // 8) * 8
    cos_step, sin_step = unit_circle(FINE * lax.broadcasted_iota(jnp.int32, (steps, 1), 0) * frequency)
    spot = slice(far * width, (far + 1) * width)

    def write(block, cosine, sine):
        if 0 <= block < blocks:
            cos_ref[near, block * FINE : (block + 1) * FINE, spot] = cosine.astype(bf16)
            sin_ref[near, block * FINE : (block + 1) * FINE, spot] = sine.astype(bf16)

    write(middle, cos_mid, sin_mid)
    for away in range(1, middle + 1):
        c = cos_step[away : away + 1]
        s = sin_step[away : away + 1]
        cc, ss, sc, cs = cos_mid * c, sin_mid * s, sin_mid * c, cos_mid * s
        write(middle + away, cc - ss, sc + cs)
        write(middle - away, cc + ss, sc - cs)


LIMIT = 8 << 20
OPENING_LIMIT = 12 << 20


def turned(values, cosine, sine, scale):
    half = values.shape[0] // 2
    with_cos = jnp.dot(values, cosine, preferred_element_type=f32)
    with_sin = jnp.dot(values, sine, preferred_element_type=f32)
    real = ((with_cos[:half] + with_sin[half:]) * scale).astype(bf16)
    imag = ((with_cos[half:] - with_sin[:half]) * scale).astype(bf16)
    return real, imag


def store_both(outs, far, real, imag):
    depth = real.shape[0] // 2
    for i, out in enumerate(outs):
        out[far, 0] = real[i * depth : (i + 1) * depth]
        out[far, 1] = imag[i * depth : (i + 1) * depth]


def opening_kernel(lay, scale, info, place, data, away, keep, cos_ref, sin_ref):
    width = away.shape[-1]
    cores = (1 - place[1], place[1])
    values = jnp.concatenate([data[part, core] for part in range(2) for core in cores], axis=0)
    fill = functools.partial(table_tile, lay, info, place, cos_ref, sin_ref, width=width)
    fill(0, 0)
    for far in range(lay.far):
        spot = slice(far * width, (far + 1) * width)
        store_both((away, keep), far, *turned(values, cos_ref[0, :, spot], sin_ref[0, :, spot], scale))
        if far + 1 < lay.far:
            fill(0, far + 1)
        fill(1, far)


def opening(lay, scale, info, place, data, width):
    depth, rows = data.shape[-2:]
    total = lay.far * width
    half = jax.ShapeDtypeStruct((lay.far, 2, depth, width), bf16)
    return pl.pallas_call(
        functools.partial(opening_kernel, lay, scale),
        out_shape=[half] * 2 + [pltpu.VMEM((2, rows, total), bf16)] * 2,
        in_specs=[SCALARS] * 2 + [WHOLE],
        out_specs=[WHOLE] * 4,
        compiler_params=pltpu.CompilerParams(vmem_limit_bytes=OPENING_LIMIT),
        cost_estimate=pl.CostEstimate(
            flops=16 * depth * rows * total + 16 * rows * total,
            transcendentals=0,
            bytes_accessed=8 * rows * total,
        ),
        name="opening",
    )(info, place, data)


def closing_kernel(lay, scale, place, data, cos_ref, sin_ref, away, keep):
    width = away.shape[-1]

    def tile(far, carry):
        spot = pl.ds(far * width, width)
        cores = (1 - place[1], place[1])
        values = jnp.concatenate([data[part, place[0], core] for part in range(2) for core in cores], axis=0)
        store_both((away, keep), far, *turned(values, cos_ref[1, :, spot], sin_ref[1, :, spot], scale))
        return carry

    lax.fori_loop(0, lay.far, tile, 0, unroll=True)


def side_kernel(lay, scale, first, other, place, data, cos_ref, sin_ref, out):
    width = out.shape[-1]
    core = 1 - place[1] if other else place[1]
    mine = jnp.where(core == 0, first, 1 - first)
    digit = jnp.where(mine == 1, place[0], 1 - place[0])
    near = 1 - mine

    def tile(far, carry):
        spot = pl.ds(far * width, width)
        values = jnp.concatenate([data[part, digit, core] for part in range(2)], axis=0)
        real, imag = turned(values, cos_ref[near, :, spot], sin_ref[near, :, spot], scale)
        out[far, 0] = real
        out[far, 1] = imag
        return carry

    lax.fori_loop(0, lay.far, tile, 0, unroll=True)


def piece(lay, kernel, count, place, data, tables, width):
    depth = data.shape[-2]
    return pl.pallas_call(
        kernel,
        out_shape=[jax.ShapeDtypeStruct((lay.far, 2, depth, width), bf16)] * count,
        in_specs=[SCALARS] + [WHOLE] * 3,
        out_specs=[WHOLE] * count,
        compiler_params=pltpu.CompilerParams(vmem_limit_bytes=LIMIT),
        name="piece",
    )(place, data, *tables)


def blocks_kernel(lay, place, held, *refs):
    parts = refs[: -lay.far]
    for shift, out in enumerate(refs[-lay.far :]):
        far = lax.rem(place[2] + shift, lay.far)
        out[...] = total_of(held[far], *[part[far] for part in parts]).astype(out.dtype)


def blocks(lay, place, held, *parts):
    shape = held.shape[1:]
    types = [f32] + [bf16] * (lay.far - 1)
    return pl.pallas_call(
        functools.partial(blocks_kernel, lay),
        out_shape=[jax.ShapeDtypeStruct(shape, kind) for kind in types],
        in_specs=[SCALARS] + [WHOLE] * (1 + len(parts)),
        out_specs=[WHOLE] * lay.far,
        compiler_params=pltpu.CompilerParams(vmem_limit_bytes=LIMIT),
        name="blocks",
    )(place, held, *parts)


def fill_left(lay, place, left, own, other):
    width = own.shape[-1]
    for i, source in enumerate((own, other)):
        core = place[1] if i == 0 else 1 - place[1]
        for third in range(lay.far):
            far = lax.rem(place[2] - third + lay.far, lay.far)
            spot = pl.ds(pl.multiple_of(far * width, width), width)
            for part in range(2):
                left[core, part, :, spot] = source[third, part]


def back(values, cos_ref, sin_ref, near, spot):
    contract = (((1,), (1,)), ((), ()))
    with_cos = lax.dot_general(values, cos_ref[near, spot], contract, preferred_element_type=f32)
    with_sin = lax.dot_general(values, sin_ref[near, spot], contract, preferred_element_type=f32)
    half = values.shape[0] // 2
    return with_cos[:half] - with_sin[half:], with_cos[half:] + with_sin[:half]


def rows_of(left, cores):
    values = [left[core, part] for part in range(2) for core in cores]
    return jnp.concatenate(values, axis=0)


def begin_kernel(lay, step, place, own, other, cos_ref, sin_ref, total, left):
    fill_left(lay, place, left, own, other)
    depth = left.shape[2]

    def tile(t, carry):
        spot = pl.ds(t * step, step)
        real, imag = back(rows_of(left, (0, 1)), cos_ref, sin_ref, 1, spot)
        for core in range(2):
            total[core, 0, :, spot] = real[core * depth : (core + 1) * depth]
            total[core, 1, :, spot] = imag[core * depth : (core + 1) * depth]
        return carry

    lax.fori_loop(0, cos_ref.shape[1] // step, tile, 0, unroll=True)


def begin(lay, pair, tables, place):
    _, rows, total = tables[0].shape
    depth = pair[0].shape[-2]
    return pl.pallas_call(
        functools.partial(begin_kernel, lay, tile_of(rows)),
        out_shape=pltpu.VMEM((2, 2, depth, rows), f32),
        in_specs=[SCALARS] + [WHOLE] * 4,
        out_specs=WHOLE,
        scratch_shapes=[pltpu.VMEM((2, 2, depth, total), bf16)],
        compiler_params=pltpu.CompilerParams(vmem_limit_bytes=LIMIT),
        name="begin",
    )(place, *pair, *tables)


def tile_of(rows):
    return 512 if rows % 512 == 0 else rows


def middle_kernel(lay, scale, ending, place, own, other, cos_ref, sin_ref, total, *refs):
    *_, out, begun, left, ready, sent = refs
    fill_left(lay, place, left, own, other)
    slots, *_, step = ready.shape
    copies = []
    for t in range(slots):
        spot = pl.ds(t * step, step)
        real, imag = back(rows_of(left, (ending,)), cos_ref, sin_ref, 0, spot)
        ready[t, 0, 0] = ((total[ending, 0, :, spot] + real) * scale).astype(bf16)
        ready[t, 1, 0] = ((total[ending, 1, :, spot] + imag) * scale).astype(bf16)
        target = out.at[:, place[0], ending : ending + 1, :, spot]
        copies.append(pltpu.make_async_copy(ready.at[t], target, sent.at[t]))
        copies[-1].start()
        real, imag = back(rows_of(left, (1 - ending,)), cos_ref, sin_ref, 1, spot)
        begun[0, :, spot] = real
        begun[1, :, spot] = imag
    for copy in copies:
        copy.wait()


def finish_kernel(lay, scale, place, own, other, cos_ref, sin_ref, *refs):
    *totals, _, out, left, ready, sent = refs
    fill_left(lay, place, left, own, other)
    depth = left.shape[2]
    slots, *_, step = ready.shape
    copies = []
    for t in range(slots):
        spot = pl.ds(t * step, step)
        real, imag = back(rows_of(left, (0, 1)), cos_ref, sin_ref, 0, spot)
        for core, total in enumerate(totals):
            block = slice(core * depth, (core + 1) * depth)
            ready[t, 0, core] = ((total[0, :, spot] + real[block]) * scale).astype(bf16)
            ready[t, 1, core] = ((total[1, :, spot] + imag[block]) * scale).astype(bf16)
        target = out.at[:, 1 - place[0], :, :, spot]
        copies.append(pltpu.make_async_copy(ready.at[t], target, sent.at[t]))
        copies[-1].start()
    for copy in copies:
        copy.wait()


OUT_SLOTS = 2


def written(lay, kernel, place, operands, earlier, cores, begun):
    _, rows, cells = operands[2].shape
    depth = operands[0].shape[-2]
    step = rows // OUT_SLOTS if rows % (OUT_SLOTS * 128) == 0 else rows
    specs = [SCALARS] + [WHOLE] * len(operands)
    if earlier is not None:
        operands = [*operands, earlier]
        specs.append(pl.BlockSpec(memory_space=pl.ANY))
    slots = rows // step
    return pl.pallas_call(
        kernel,
        out_shape=[jax.ShapeDtypeStruct((2, lay.high, 2, depth, rows), bf16)]
        + [pltpu.VMEM((2, depth, rows), f32)] * begun,
        in_specs=specs,
        out_specs=[pl.BlockSpec(memory_space=pl.ANY)] + [WHOLE] * begun,
        scratch_shapes=[
            pltpu.VMEM((2, 2, depth, cells), bf16),
            pltpu.VMEM((slots, 2, cores, depth, step), bf16),
            pltpu.SemaphoreType.DMA((slots,)),
        ],
        input_output_aliases={} if earlier is None else {len(operands): 0},
        compiler_params=pltpu.CompilerParams(vmem_limit_bytes=LIMIT),
    )(place, *operands)


def middle(lay, pair, tables, total, place, ending, scale, earlier=None):
    return written(
        lay, functools.partial(middle_kernel, lay, scale, ending), place, [*pair, *tables, total], earlier, 1, 1
    )


def finish(lay, pair, tables, totals, place, scale, earlier):
    return written(
        lay, functools.partial(finish_kernel, lay, scale), place, [*pair, *tables, *totals], earlier, 2, 0
    )[0]


def in_pieces(lay, facets, offsets, visibilities, weights, mask):
    high, core, far, near = lay.place()
    _, _, _, rows = facets.shape
    _, depth, width = visibilities.shape
    facet_index = lax.axis_index("facet")
    all_rows = rows * lay.strips
    base = lax.axis_index("strip") * rows + facet_index % FROWS * all_rows + NG // 2
    info = jnp.concatenate([jnp.stack([base, core]).astype(jnp.int32), offsets])
    place = jnp.stack([high, core, far, near]).astype(jnp.int32)
    scale = 1.0 / math.sqrt(all_rows)
    data = facets.reshape(2, lay.high, lay.cores, depth, rows)

    def sent(stage, *values):
        return lay.send(values[0] if len(values) == 1 else total_of(*values).astype(bf16), stage, 1)

    def side(first, other):
        return piece(lay, functools.partial(side_kernel, lay, scale, first, other), 1, place, data, tables, width)[0]

    others = lax.dynamic_index_in_dim(data, 1 - high, 1, keepdims=False)
    away, keep, *tables = opening(lay, scale, info, place, others, width)
    cross = sent("core", away)
    away = side(0, True)
    first_a = sent("first", keep, cross)
    cross = sent("core", away)
    keep = side(0, False)
    first_b = sent("first", keep, cross)
    away = side(1, True)
    cross = sent("core", away)
    keep = side(1, False)
    second = sent("second", keep, cross, first_a)
    away, keep = piece(lay, functools.partial(closing_kernel, lay, scale), 2, place, data, tables, width)
    cross = sent("core", away)
    own, *others = blocks(lay, place, keep, cross, first_b, second)
    model = total_of(own, *[lay.send(value, "far", 1 + i) for i, value in enumerate(others)])

    factor = weights * mask.astype(f32)
    residual = (factor[None] * (visibilities - model)).astype(bf16)

    def paired(value):
        return [value, sent("core", value)]

    arrived = [residual]
    for shift in range(1, lay.far):
        arrived.append(lay.send(residual, "far", shift))
    corner = jnp.stack(arrived)
    over_second = sent("second", corner)
    corners = paired(corner)
    total = begin(lay, corners, tables, place)
    over_first = sent("first", corner)
    over_both = sent("first", over_second)
    seconds = paired(over_second)
    update, begun_one = middle(lay, seconds, tables, total, place, 0, scale)
    firsts = paired(over_first)
    update, begun_zero = middle(lay, firsts, tables, total, place, 1, scale, update)
    boths = paired(over_both)
    update = finish(lay, boths, tables, (begun_zero, begun_one), place, scale, update)
    return update.reshape(facets.shape)


def on_device(lay, *arrays):
    if lay.fast:
        return in_pieces(lay, *arrays)
    return in_stages(lay, *arrays)


def solution(mesh):
    placed = (
        P("facet", None, None, "strip"),
        P(),
        P(None, "strip", "facet"),
        P("strip", "facet"),
        P("strip", "facet"),
    )
    lay = Layout(mesh)
    return jax.shard_map(
        functools.partial(on_device, lay),
        mesh=mesh,
        in_specs=placed,
        out_specs=P("facet", None, None, "strip"),
        check_vma=False,
    )
```
